128 devices in a mesh: dom: 64 (over y, x, z), seed: 2 (over core).
Axes of the slice: x: 4, y: 4, z: 4, core: 2. Of those that a mesh axis runs over, the one named last changes fastest.
Arguments:
- rank_in: float32 [128, 1048576], P('seed', 'dom'), as said below
- band_tiles: bfloat16 [8192, 3, 128, 128], P('dom'), as said below
- off_tiles: bfloat16 [32768, 128, 128], P('dom'), as said below
- tile_src: int32 [64, 512], P('dom'), may hold values from 0 to 8191, as said below
- tile_row: int32 [64, 512], P('dom'), may hold values from 0 to 127
- tile_count: int32 [64], P('dom'), may hold values from 256 to 512, as said below
- seed_ids: int32 [128], P('seed'), may hold values from 0 to 1048575
- dangling: int32 [1048576], P('dom'), may hold values 0 or 1
Outputs:
- rank_out: float32 [128, 1048576], P('seed', 'dom')
- change: float32 [3, 128], P(None, 'seed')
- total_change: float32 [3], replicated
- seed_score: float32 [128], P('seed')
The draws below stay inside these ranges and needn't reach their ends.
Inputs may be any that keep to these rules, and one draw needn't show every extreme that they name: `rank_in`: positive. `band_tiles`: nonnegative transition weights. `off_tiles`: nonnegative transition weights. `tile_src`: every source block is held by another index of dom than the tile; the live tiles of one index of dom read at most 2 distinct blocks held by any one other index. The first tile_count[g] slots of index g are live, the rest are padding.
All inputs are finite; a program needn't handle non-finite values. No bound on the sum of `dangling` on one device may be relied on, other than what follows from the above.
Results may differ from the reference program's by a relative error of at most 0.0003.
Values may be sent and summed in bfloat16 or wider, within the bound.
No kernel may reach another device: no remote copies, remote signals or barrier semaphores. Data moves between devices by JAX's collectives and lax.ppermute only.
A program may use at most 192 MiB of HBM per device.

```python
import math
import jax
import jax.numpy as jnp
from jax import lax

S = 128
BLK = 128
NB_DEV = 128
CAP = 2
ITERS = 3
KT = 512
TILES = 32768
NBLK = 8192
NV = 1048576
N_DOM = 64


def pick_device(key):
    return jax.random.randint(jax.random.fold_in(key, 7), (), 0, N_DOM)


def draw_tile_count(key, part):
    counts = jax.random.randint(jax.random.fold_in(key, 11), (N_DOM,), KT // 2, KT + 1)
    chosen = pick_device(key)
    return jnp.where(jnp.arange(N_DOM) == chosen, KT, counts).astype(jnp.int32)


def draw_tile_src(key, part):
    step_key = jax.random.fold_in(key, 21)
    offset_key = jax.random.fold_in(key, 22)
    within_key = jax.random.fold_in(key, 23)
    device = jnp.arange(N_DOM, dtype=jnp.int32)[:, None]
    slots = jnp.arange(KT, dtype=jnp.int32)[None, :]
    stride = jax.random.randint(step_key, (N_DOM, KT), 1, N_DOM)
    holder = (device + stride) % N_DOM
    offset = jax.random.randint(offset_key, (N_DOM, N_DOM), 0, NB_DEV)
    within = jax.random.randint(within_key, (N_DOM, KT), 0, CAP)
    chosen = pick_device(key)
    forced = jnp.logical_and(device == chosen, slots < CAP * (N_DOM - 1))
    holder = jnp.where(forced, (chosen + 1 + slots // CAP) % N_DOM, holder)
    within = jnp.where(forced, slots % CAP, within)
    start = jnp.take_along_axis(offset, holder, axis=1)
    inside = (start + within) % NB_DEV
    return (holder * NB_DEV + inside).astype(jnp.int32)


def sparse_tiles(key, shape):
    keep = (jax.random.uniform(jax.random.fold_in(key, 31), shape) < 0.25).astype(jnp.float32)
    value_key = jax.random.fold_in(key, 32)
    values = jnp.exp(jax.random.uniform(value_key, shape, jnp.float32, math.log(0.1), math.log(10.0)))
    scale = 1.0 / (0.54 * BLK * (3.0 + KT / NB_DEV))
    return (keep * values * scale).astype(jnp.bfloat16)


def draw_band_tiles(key, part):
    return sparse_tiles(key, (NBLK, 3, BLK, BLK))


def draw_off_tiles(key, part):
    return sparse_tiles(jax.random.fold_in(key, 5), (TILES, BLK, BLK))


def draw_rank_in(key, part):
    row_scale = jnp.exp(jax.random.uniform(jax.random.fold_in(key, 41), (1, NV), jnp.float32, math.log(0.3), math.log(3.0)))
    col_scale = jnp.exp(jax.random.uniform(jax.random.fold_in(key, 42), (S, 1), jnp.float32, math.log(0.5), math.log(2.0)))
    rising = 1.0 + 2.0 * jnp.arange(NV, dtype=jnp.float32)[None, :] / NV
    entry_key = jax.random.fold_in(key, 43)
    entry = jnp.exp(jax.random.uniform(entry_key, (S, NV), jnp.float32, math.log(0.5), math.log(2.0)))
    return row_scale * col_scale * entry * rising


def with_ends(drawn, rng, low, high):
    longest = drawn.shape.index(max(drawn.shape))
    spots = []
    for shift in (0, 1):
        where = [jax.random.randint(jax.random.fold_in(rng, axis), (), 0, length) for axis, length in enumerate(drawn.shape)]
        where[longest] = (where[longest] + shift) % drawn.shape[longest]
        spots.append(tuple(where))
    return drawn.at[spots[0]].set(low).at[spots[1]].set(high)


def setup_inputs(seed: int = 0) -> dict:
    keys = jax.random.split(jax.random.key(seed), 9)
    return {
        "rank_in": draw_rank_in(jax.random.fold_in(keys[8], 71), 0),
        "band_tiles": draw_band_tiles(jax.random.fold_in(keys[8], 71), 0),
        "off_tiles": draw_off_tiles(jax.random.fold_in(keys[8], 71), 0),
        "tile_src": draw_tile_src(jax.random.fold_in(keys[8], 71), 0),
        "tile_row": with_ends(jax.random.randint(keys[4], (N_DOM, KT), 0, NB_DEV), jax.random.fold_in(keys[4], 1), 0, NB_DEV - 1).astype(jnp.int32),
        "tile_count": draw_tile_count(jax.random.fold_in(keys[8], 71), 0),
        "seed_ids": with_ends(jax.random.randint(keys[6], (S,), 0, NV), jax.random.fold_in(keys[6], 1), 0, NV - 1).astype(jnp.int32),
        "dangling": with_ends((jax.random.randint(keys[7], (NV,), 0, 4) < 1).astype(jnp.int32), jax.random.fold_in(keys[7], 1), 0, 1),
    }


DAMP = 0.85


def reference(rank_in, band_tiles, off_tiles, tile_src, tile_row, tile_count, seed_ids, dangling):
    dead_ends = dangling.astype(jnp.float32)
    keep_share = 1.0 - dead_ends
    vertices = jnp.arange(NV, dtype=jnp.int32)
    live_slots = (jnp.arange(KT, dtype=jnp.int32)[None, :] < tile_count[:, None]).reshape(-1)
    targets = (jnp.arange(N_DOM, dtype=jnp.int32)[:, None] * NB_DEV + tile_row).reshape(-1)
    targets = jnp.where(live_slots, targets, NBLK).astype(jnp.int32)
    sources = tile_src.reshape(-1).astype(jnp.int32)
    band_wide = band_tiles.astype(jnp.float32)
    off_wide = off_tiles.astype(jnp.float32)
    highest = lax.Precision.HIGHEST

    def one_group(packed):
        rank_now, seed_group = packed
        seed_mask = (seed_group[:, None] == vertices[None, :]).astype(jnp.float32)
        restart = (1.0 - DAMP) * seed_mask
        changes = []
        for iteration in range(ITERS):
            dead_mass = jnp.sum(rank_now * dead_ends[None, :], axis=1)
            rounded = lax.optimization_barrier((rank_now * keep_share[None, :]).astype(jnp.bfloat16))
            source = rounded.astype(jnp.float32).reshape(rank_now.shape[0], NBLK, BLK)
            padded = jnp.pad(source, ((0, 0), (1, 1), (0, 0)))
            banded = jnp.einsum("sbj,bij->sbi", padded[:, 0:NBLK], band_wide[:, 0], precision=highest)
            banded = banded + jnp.einsum("sbj,bij->sbi", padded[:, 1:NBLK + 1], band_wide[:, 1], precision=highest)
            banded = banded + jnp.einsum("sbj,bij->sbi", padded[:, 2:NBLK + 2], band_wide[:, 2], precision=highest)
            operands = jnp.take(source, sources, axis=1)
            products = jnp.einsum("stj,tij->sti", operands, off_wide, precision=highest)
            remote = jax.ops.segment_sum(jnp.moveaxis(products, 1, 0), targets, num_segments=NBLK + 1)[:NBLK]
            linked = banded + jnp.moveaxis(remote, 0, 1)
            updated = DAMP * (linked.reshape(rank_now.shape[0], NV) + dead_mass[:, None] / NV) + restart
            changes.append(jnp.sum(jnp.abs(updated - rank_now), axis=1) / NV)
            rank_now = updated
        score = jnp.sum(rank_now * seed_mask, axis=1)
        return rank_now, jnp.stack(changes), score

    group_count = 8
    ranks, changes, scores = lax.map(one_group, (rank_in.reshape(group_count, S // group_count, NV), seed_ids.reshape(group_count, S // group_count)))
    rank_out = ranks.reshape(S, NV)
    change = jnp.transpose(changes, (1, 0, 2)).reshape(ITERS, S)
    total_change = jnp.sum(change, axis=1) / S
    seed_score = scores.reshape(S)
    return rank_out, change, total_change, seed_score
```

```python
import functools

import jax
import jax.numpy as jnp
from jax import lax
from jax.experimental import pallas as pl
from jax.experimental.pallas import tpu as pltpu
from jax.sharding import PartitionSpec as P

CAP = 2
ITERS = 3
DAMP = 0.85

BF16 = jnp.bfloat16
F32 = jnp.float32
I32 = jnp.int32
VMEM = pltpu.VMEM
NT = (((1,), (1,)), ((), ()))
SLAB = 8
PARAMS = pltpu.CompilerParams(vmem_limit_bytes=52 << 20)


def vmem():
    return pl.BlockSpec(memory_space=pltpu.VMEM)


def smem():
    return pl.BlockSpec(memory_space=pltpu.SMEM)


def anywhere():
    return pl.BlockSpec(memory_space=pl.ANY)


def shaped(shape, dtype):
    return jax.ShapeDtypeStruct(shape, dtype)


def dot_nt(x, w):
    return lax.dot_general(x, w, NT, preferred_element_type=F32)


def plan_kernel(peers, blocks, count_ref, src_ref, row_ref, request_ref, slot_ref, target_ref):
    slots = src_ref.shape[1]
    ids = src_ref[...]
    live = lax.broadcasted_iota(I32, (1, slots), 1) < count_ref[0]
    holder = ids // blocks
    inside = (ids - holder * blocks).astype(F32)
    peer = lax.broadcasted_iota(I32, (peers, slots), 0)
    held = jnp.broadcast_to(holder, (peers, slots)) == peer
    asked = jnp.logical_and(held, jnp.broadcast_to(live, (peers, slots)))
    block_of = jnp.broadcast_to(inside, (peers, slots))
    low = jnp.min(jnp.where(asked, block_of, float(blocks - 1)), axis=1, keepdims=True)
    high = jnp.max(jnp.where(asked, block_of, 0.0), axis=1, keepdims=True)
    lane = lax.broadcasted_iota(I32, request_ref.shape, 1)
    request_ref[...] = jnp.where(lane == 0, low, high).astype(I32)
    low_of = jnp.sum(jnp.where(held, low, 0.0), axis=0, keepdims=True)
    slot_ref[...] = holder * CAP + jnp.where(inside == low_of, 0, 1)
    target_ref[...] = jnp.where(live, row_ref[...], blocks)


def plan(tile_count, tile_src, tile_row, peers, blocks):
    slots = tile_src.shape[1]
    return pl.pallas_call(
        functools.partial(plan_kernel, peers, blocks),
        out_shape=(shaped((peers, 128), I32), shaped((1, slots), I32), shaped((1, slots), I32)),
        in_specs=[smem(), vmem(), vmem()],
        out_specs=(vmem(), vmem(), vmem()),
        name="plan",
    )(tile_count, tile_src, tile_row)


def eye(rows):
    return lax.broadcasted_iota(I32, (rows, 128), 0) == lax.broadcasted_iota(I32, (rows, 128), 1)


def to_row(column):
    return jnp.sum(jnp.where(eye(column.shape[0]), column, 0.0), axis=0, keepdims=True)


def to_column(row, seeds):
    return jnp.sum(jnp.where(eye(seeds), row, 0.0), axis=1, keepdims=True)


def mass_slab(mass):
    row = to_row(jnp.sum(mass, axis=1, keepdims=True))
    high = row.astype(BF16).astype(F32)
    rest = row - high
    middle = rest.astype(BF16).astype(F32)
    low = rest - middle
    at = lax.broadcasted_iota(I32, (SLAB, 128), 0)
    slab = jnp.where(at == 0, high, jnp.where(at == 1, middle, jnp.where(at == 2, low, 0.0)))
    return slab.astype(BF16)


def prep_kernel(rank_hbm, dangling_ref, source_ref, slab_ref, head_ref, tail_ref, rank, sem):
    blocks, seeds, width = source_ref.shape
    chunks = sem.shape[0]
    per = blocks // chunks

    def fetch(c):
        cols = pl.ds(c * per * width, per * width)
        return pltpu.make_async_copy(rank_hbm.at[:, cols], rank.at[:, cols], sem.at[c])

    for c in range(chunks):
        fetch(c).start()
    mass = jnp.zeros((seeds, width), F32)
    for c in range(chunks):
        fetch(c).wait()
        for b in range(c * per, (c + 1) * per):
            old = rank[:, b * width : (b + 1) * width]
            dead = jnp.broadcast_to(dangling_ref[b : b + 1, :], (seeds, width)) != 0
            kept = jnp.where(dead, 0.0, old)
            mass += old - kept
            source_ref[b] = kept.astype(BF16)
    slab_ref[...] = mass_slab(mass)
    head_ref[...] = source_ref[0]
    tail_ref[...] = source_ref[blocks - 1]


def prep(rank, dangling, blocks):
    seeds = rank.shape[0]
    width = rank.shape[1] // blocks
    edge = shaped((seeds, width), BF16)
    return pl.pallas_call(
        prep_kernel,
        out_shape=(shaped((blocks, seeds, width), BF16), shaped((SLAB, 128), BF16), edge, edge),
        in_specs=[anywhere(), vmem()],
        out_specs=(vmem(),) * 4,
        scratch_shapes=[VMEM(rank.shape, F32), pltpu.SemaphoreType.DMA((8,))],
        compiler_params=PARAMS,
        name="prep",
    )(rank, dangling)


def pack(wanted, source, slab, message, out_hbm, sem):
    peers, _, _ = message.shape
    seeds = source.shape[1]
    parts = sem.shape[0]
    per = peers // parts

    def send(c):
        span = pl.ds(c * per, per)
        return pltpu.make_async_copy(message.at[span], out_hbm.at[span], sem.at[c])

    for c in range(parts):

        def one(p, carry):
            for k in range(CAP):
                message[p, k * seeds : (k + 1) * seeds, :] = source[wanted[p, k]]
            message[p, CAP * seeds :, :] = slab
            return carry

        lax.fori_loop(c * per, (c + 1) * per, one, 0, unroll=4)
        send(c).start()
    for c in range(parts):
        send(c).wait()


def pack_kernel(wanted_ref, source_ref, slab_ref, out_hbm, message, sem):
    pack(wanted_ref, source_ref, slab_ref[...], message, out_hbm, sem)


def pack_first(wanted, source, slab, peers):
    _, seeds, width = source.shape
    shape = (peers, CAP * seeds + SLAB, width)
    return pl.pallas_call(
        pack_kernel,
        out_shape=shaped(shape, BF16),
        in_specs=[smem(), vmem(), vmem()],
        out_specs=anywhere(),
        scratch_shapes=[VMEM(shape, BF16), pltpu.SemaphoreType.DMA((4,))],
        compiler_params=PARAMS,
        name="pack",
    )(wanted, source, slab)


def band_kernel(source_hbm, left_ref, right_ref, tiles_hbm, out_hbm, source, tiles, banded, sem, source_sem, out_sem):
    blocks, seeds, width = banded.shape
    chunks = sem.shape[0]
    per = blocks // chunks

    def fetch(c):
        span = pl.ds(c * per, per)
        return pltpu.make_async_copy(tiles_hbm.at[span], tiles.at[span], sem.at[c])

    def flush(c):
        span = pl.ds(c * per, per)
        return pltpu.make_async_copy(banded.at[span], out_hbm.at[span], out_sem.at[c])

    own = pltpu.make_async_copy(source_hbm, source.at[pl.ds(1, blocks)], source_sem)
    own.start()
    for c in range(chunks):
        fetch(c).start()
    source[0] = left_ref[...]
    source[blocks + 1] = right_ref[...]
    own.wait()
    for c in range(chunks):
        fetch(c).wait()
        for b in range(c * per, (c + 1) * per):
            x = jnp.concatenate([source[b], source[b + 1], source[b + 2]], axis=1)
            w = jnp.concatenate([tiles[b, 0], tiles[b, 1], tiles[b, 2]], axis=1)
            banded[b] = dot_nt(x, w)
        flush(c).start()
    for c in range(chunks):
        flush(c).wait()


def band(source, left, right, tiles):
    blocks, seeds, width = source.shape
    return pl.pallas_call(
        band_kernel,
        out_shape=shaped((blocks, seeds, width), F32),
        in_specs=[anywhere(), vmem(), vmem(), anywhere()],
        out_specs=anywhere(),
        scratch_shapes=[
            VMEM((blocks + 2, seeds, width), BF16),
            VMEM(tiles.shape, BF16),
            VMEM((blocks, seeds, width), F32),
            pltpu.SemaphoreType.DMA((8,)),
            pltpu.SemaphoreType.DMA,
            pltpu.SemaphoreType.DMA((8,)),
        ],
        compiler_params=PARAMS,
        name="band",
    )(source, left, right, tiles)


UNROLL = 32


def finish_kernel(last, vertices, *refs):
    (first_ref, count_ref, slot_ref, target_ref, wanted_ref, seed_ref, dangling_ref) = refs[:7]
    fetched_hbm, banded_hbm, rank_hbm, tiles_hbm = refs[7:11]
    if last:
        next_hbm, stats_ref = refs[11:13]
        scratch = refs[13:]
    else:
        next_hbm, stats_ref, source, head_ref, tail_ref, message_hbm, message, send_sem = refs[11:19]
        scratch = refs[19:]
    fetched, tiles, acc, rank, nxt, sem, tile_sem, rank_sem, out_sem = scratch
    blocks = acc.shape[0] - 1
    seeds, width = acc.shape[1:]
    peers = fetched.shape[0]
    chunks = tile_sem.shape[0]
    per = tiles.shape[0] // chunks
    parts = rank_sem.shape[0]
    span = blocks // parts

    def tile_copy(c):
        at = pl.ds(c * per, per)
        return pltpu.make_async_copy(tiles_hbm.at[at], tiles.at[at], tile_sem.at[c])

    def rank_copy(c):
        cols = pl.ds(c * span * width, span * width)
        return pltpu.make_async_copy(rank_hbm.at[:, cols], rank.at[:, cols], rank_sem.at[c])

    def rank_store(c):
        cols = pl.ds(c * span * width, span * width)
        return pltpu.make_async_copy(nxt.at[:, cols], next_hbm.at[:, cols], out_sem.at[c])

    got = pltpu.make_async_copy(fetched_hbm, fetched, sem.at[0])
    base = pltpu.make_async_copy(banded_hbm, acc.at[pl.ds(0, blocks)], sem.at[1])
    got.start()
    base.start()
    for c in range(chunks):
        tile_copy(c).start()
    for c in range(parts):
        rank_copy(c).start()
    got.wait()
    slabs = fetched[:, CAP * seeds :, :].astype(F32)
    mass_row = jnp.sum(jnp.sum(slabs, axis=0), axis=0, keepdims=True)
    share = jnp.broadcast_to(to_column(mass_row, seeds) / vertices, (seeds, width))
    acc[blocks] = jnp.zeros((seeds, width), F32)
    zero = jnp.zeros((seeds, width), BF16)
    base.wait()

    def operand(t):
        slot = slot_ref[0, t]
        at = pl.multiple_of((slot % CAP) * seeds, seeds)
        return fetched[slot // CAP, pl.ds(at, seeds), :]

    def group(g, carry):
        first = g * UNROLL
        products = []
        for u in range(0, UNROLL, 2):
            one, two = first + u, first + u + 1
            x = jnp.concatenate(
                [
                    jnp.concatenate([operand(one), zero], axis=1),
                    jnp.concatenate([zero, operand(two)], axis=1),
                ],
                axis=0,
            )
            y = dot_nt(x, jnp.concatenate([tiles[one], tiles[two]], axis=1))
            products += [y[:seeds], y[seeds:]]
        for u in range(UNROLL):
            row = target_ref[0, first + u]
            acc[row] = acc[row] + products[u]
        return carry

    groups = per // UNROLL
    used = (count_ref[0] + UNROLL - 1) // UNROLL

    def chunk(c, carry):
        tile_copy(c).wait()
        lax.fori_loop(c * groups, jnp.clip(used, c * groups, (c + 1) * groups), group, 0)
        return carry

    lax.fori_loop(0, chunks, chunk, 0)

    away = jnp.broadcast_to(seed_ref[...] - first_ref[0], (seeds, width)) - lax.broadcasted_iota(
        I32, (seeds, width), 1
    )

    def update(b, carry):
        gap, other = carry
        cols = pl.ds(pl.multiple_of(b * width, width), width)
        old = rank[:, cols]
        at_seed = away == b * width
        new = DAMP * (acc[b] + share) + jnp.where(at_seed, 1.0 - DAMP, 0.0)
        nxt[:, cols] = new
        gap = gap + jnp.abs(new - old)
        if last:
            return gap, other + jnp.where(at_seed, new, 0.0)
        dead = jnp.broadcast_to(dangling_ref[pl.ds(b, 1), :], (seeds, width)) != 0
        kept = jnp.where(dead, 0.0, new)
        source[b] = kept.astype(BF16)
        return gap, other + (new - kept)

    carry = (jnp.zeros((seeds, width), F32), jnp.zeros((seeds, width), F32))
    for c in range(parts):
        rank_copy(c).wait()
        carry = lax.fori_loop(c * span, (c + 1) * span, update, carry, unroll=8)
        rank_store(c).start()
    gap, other = carry
    gap_row = to_row(jnp.sum(gap, axis=1, keepdims=True))
    if last:
        own_row = to_row(jnp.sum(other, axis=1, keepdims=True))
        stats_ref[0:1, :] = gap_row
        stats_ref[1:2, :] = own_row
    else:
        stats_ref[0:1, :] = gap_row
        stats_ref[1:2, :] = jnp.zeros((1, 128), F32)
        head_ref[...] = source[0]
        tail_ref[...] = source[blocks - 1]
        pack(wanted_ref, source, mass_slab(other), message, message_hbm, send_sem)
    for c in range(parts):
        rank_store(c).wait()


def finish(last, vertices, first, count, slot, target, wanted, seeds_at, dangling, fetched, banded, rank, tiles):
    blocks, seeds, width = banded.shape
    out_shape = [shaped(rank.shape, F32), shaped((2, 128), F32)]
    out_specs = [anywhere(), vmem()]
    extra = []
    if not last:
        edge = shaped((seeds, width), BF16)
        out_shape += [shaped((blocks, seeds, width), BF16), edge, edge, shaped(fetched.shape, BF16)]
        out_specs += [vmem(), vmem(), vmem(), anywhere()]
        extra = [VMEM(fetched.shape, BF16), pltpu.SemaphoreType.DMA((4,))]
    return pl.pallas_call(
        functools.partial(finish_kernel, last, vertices),
        out_shape=tuple(out_shape),
        in_specs=[smem()] * 5 + [vmem()] * 2 + [anywhere()] * 4,
        out_specs=tuple(out_specs),
        scratch_shapes=extra
        + [
            VMEM(fetched.shape, BF16),
            VMEM(tiles.shape, BF16),
            VMEM((blocks + 1, seeds, width), F32),
            VMEM(rank.shape, F32),
            VMEM(rank.shape, F32),
            pltpu.SemaphoreType.DMA((2,)),
            pltpu.SemaphoreType.DMA((8,)),
            pltpu.SemaphoreType.DMA((8,)),
            pltpu.SemaphoreType.DMA((8,)),
        ],
        compiler_params=PARAMS,
        name="finish",
    )(first, count, slot, target, wanted, seeds_at, dangling, fetched, banded, rank, tiles)


def stats_kernel(seeds, vertices, group_ref, got_ref, change_ref, total_ref, own_ref):
    got = got_ref[...]
    odd = lax.broadcasted_iota(I32, got.shape, 0) % 2 == 1
    one = jnp.sum(jnp.where(odd, got, 0.0), axis=0, keepdims=True)
    zero = jnp.sum(jnp.where(odd, 0.0, got), axis=0, keepdims=True)
    mine = jnp.where(group_ref[0] == 1, one, zero)
    both = one + zero
    for i in range(ITERS):
        lanes = slice(i * seeds, (i + 1) * seeds)
        change_ref[i : i + 1, :] = mine[:, lanes] / vertices
        total_ref[:, i : i + 1] = jnp.sum(both[:, lanes] / vertices, axis=1, keepdims=True) / (2 * seeds)
    own_ref[...] = mine[:, ITERS * seeds :]


def on_device(rank_in, band_tiles, off_tiles, tile_src, tile_row, tile_count, seed_ids, dangling):
    blocks, _, width, _ = band_tiles.shape
    seeds = rank_in.shape[0]
    peers = lax.axis_size("dom")
    groups = lax.axis_size("seed")
    vertices = blocks * width * peers
    first = (lax.axis_index("dom") * (blocks * width)).astype(I32).reshape(1)
    group = lax.axis_index("seed").astype(I32).reshape(1)
    dangling = dangling.reshape(blocks, width)
    seeds_at = seed_ids.reshape(seeds, 1)

    request, slot, target = plan(tile_count, tile_src, tile_row, peers, blocks)
    wanted = lax.all_to_all(request, "dom", split_axis=0, concat_axis=0, tiled=True)
    source, slab, head, tail = prep(rank_in, dangling, blocks)
    message = pack_first(wanted, source, slab, peers)
    rank = rank_in
    rows = []
    for iteration in range(ITERS):
        last = iteration + 1 == ITERS
        fetched = lax.all_to_all(message, "dom", split_axis=0, concat_axis=0, tiled=True)
        left = lax.ppermute(tail, "dom", [(i, i + 1) for i in range(peers - 1)])
        right = lax.ppermute(head, "dom", [(i + 1, i) for i in range(peers - 1)])
        banded = band(source, left, right, band_tiles)
        done = finish(
            last, vertices, first, tile_count, slot, target, wanted, seeds_at, dangling, fetched, banded, rank, off_tiles
        )
        rank, stats = done[:2]
        rows.append(stats[0:1, :seeds])
        if not last:
            source, head, tail, message = done[2:]
    rows.append(stats[1:2, :seeds])
    line = jnp.concatenate(rows, axis=1)
    got = lax.all_to_all(
        jnp.broadcast_to(line, (peers * groups, line.shape[1])),
        ("dom", "seed"),
        split_axis=0,
        concat_axis=0,
        tiled=True,
    )
    change, total, own = pl.pallas_call(
        functools.partial(stats_kernel, seeds, vertices),
        out_shape=(shaped((ITERS, seeds), F32), shaped((1, ITERS), F32), shaped((1, seeds), F32)),
        in_specs=[smem(), vmem()],
        out_specs=(vmem(),) * 3,
        name="stats",
    )(group, got)
    return (rank, change, total.reshape(ITERS), own.reshape(seeds))


def solution(mesh):
    return jax.shard_map(
        on_device,
        mesh=mesh,
        in_specs=(
            P("seed", "dom"),
            P("dom", None, None, None),
            P("dom", None, None),
            P("dom", None),
            P("dom", None),
            P("dom"),
            P("seed"),
            P("dom"),
        ),
        out_specs=(P("seed", "dom"), P(None, "seed"), P(), P("seed")),
        check_vma=False,
    )
```

```python
import functools

import jax
import jax.numpy as jnp
from jax import lax
from jax.experimental import pallas as pl
from jax.experimental.pallas import tpu as pltpu
from jax.sharding import PartitionSpec as P

CAP = 2
ITERS = 3
DAMP = 0.85

BF16 = jnp.bfloat16
F32 = jnp.float32
I32 = jnp.int32
VMEM = pltpu.VMEM
NT = (((1,), (1,)), ((), ()))
SLAB = 8
PARAMS = pltpu.CompilerParams(vmem_limit_bytes=44 << 20)
MIDDLE = pltpu.CompilerParams(vmem_limit_bytes=24 << 20)
SMALL = pltpu.CompilerParams(vmem_limit_bytes=16 << 20)


def vmem():
    return pl.BlockSpec(memory_space=pltpu.VMEM)


def smem():
    return pl.BlockSpec(memory_space=pltpu.SMEM)


def hbm():
    return pl.BlockSpec(memory_space=pltpu.HBM)


def in_hbm(shape, dtype):
    return pltpu.HBM(shape, dtype)


def off_chip(x):
    return pltpu.with_memory_space_constraint(x, pltpu.HBM)


def shaped(shape, dtype):
    return jax.ShapeDtypeStruct(shape, dtype)


def dot_nt(x, w):
    return lax.dot_general(x, w, NT, preferred_element_type=F32)


def plan_kernel(peers, blocks, count_ref, src_ref, row_ref, request_ref, slot_ref, target_ref):
    slots = src_ref.shape[1]
    ids = src_ref[...]
    live = lax.broadcasted_iota(I32, (1, slots), 1) < count_ref[0]
    holder = ids // blocks
    inside = (ids - holder * blocks).astype(F32)
    peer = lax.broadcasted_iota(I32, (peers, slots), 0)
    held = jnp.broadcast_to(holder, (peers, slots)) == peer
    asked = jnp.logical_and(held, jnp.broadcast_to(live, (peers, slots)))
    block_of = jnp.broadcast_to(inside, (peers, slots))
    low = jnp.min(jnp.where(asked, block_of, float(blocks - 1)), axis=1, keepdims=True)
    high = jnp.max(jnp.where(asked, block_of, 0.0), axis=1, keepdims=True)
    lane = lax.broadcasted_iota(I32, request_ref.shape, 1)
    request_ref[...] = jnp.where(lane == 0, low, high).astype(I32)
    low_of = jnp.sum(jnp.where(held, low, 0.0), axis=0, keepdims=True)
    slot_ref[...] = holder * CAP + jnp.where(inside == low_of, 0, 1)
    target_ref[...] = jnp.where(live, row_ref[...], blocks)


def plan(tile_count, tile_src, tile_row, peers, blocks):
    slots = tile_src.shape[1]
    return pl.pallas_call(
        functools.partial(plan_kernel, peers, blocks),
        out_shape=(shaped((peers, 128), I32), shaped((1, slots), I32), shaped((1, slots), I32)),
        in_specs=[smem(), vmem(), vmem()],
        out_specs=(vmem(), vmem(), vmem()),
        name="plan",
    )(tile_count, tile_src, tile_row)


def eye(rows):
    return lax.broadcasted_iota(I32, (rows, 128), 0) == lax.broadcasted_iota(I32, (rows, 128), 1)


def to_row(column):
    return jnp.sum(jnp.where(eye(column.shape[0]), column, 0.0), axis=0, keepdims=True)


def to_column(row, seeds):
    return jnp.sum(jnp.where(eye(seeds), row, 0.0), axis=1, keepdims=True)


def mass_slab(mass):
    row = to_row(jnp.sum(mass, axis=1, keepdims=True))
    high = row.astype(BF16).astype(F32)
    rest = row - high
    middle = rest.astype(BF16).astype(F32)
    low = rest - middle
    at = lax.broadcasted_iota(I32, (SLAB, 128), 0)
    slab = jnp.where(at == 0, high, jnp.where(at == 1, middle, jnp.where(at == 2, low, 0.0)))
    return slab.astype(BF16)


def prep_kernel(rank_hbm, dangling_ref, source_ref, slab_ref, head_ref, tail_ref, rank, sem):
    blocks, seeds, width = source_ref.shape
    chunks = sem.shape[0]
    per = blocks // chunks

    def fetch(c):
        cols = pl.ds(c * per * width, per * width)
        return pltpu.make_async_copy(rank_hbm.at[:, cols], rank.at[:, cols], sem.at[c])

    for c in range(chunks):
        fetch(c).start()
    mass = jnp.zeros((seeds, width), F32)
    for c in range(chunks):
        fetch(c).wait()
        for b in range(c * per, (c + 1) * per):
            old = rank[:, b * width : (b + 1) * width]
            dead = jnp.broadcast_to(dangling_ref[b : b + 1, :], (seeds, width)) != 0
            kept = jnp.where(dead, 0.0, old)
            mass += old - kept
            source_ref[b] = kept.astype(BF16)
    slab_ref[...] = mass_slab(mass)
    head_ref[...] = source_ref[0]
    tail_ref[...] = source_ref[blocks - 1]


def prep(rank, dangling, blocks):
    seeds = rank.shape[0]
    width = rank.shape[1] // blocks
    edge = shaped((seeds, width), BF16)
    return pl.pallas_call(
        prep_kernel,
        out_shape=(shaped((blocks, seeds, width), BF16), shaped((SLAB, 128), BF16), edge, edge),
        in_specs=[hbm(), vmem()],
        out_specs=(vmem(),) * 4,
        scratch_shapes=[VMEM(rank.shape, F32), pltpu.SemaphoreType.DMA((8,))],
        compiler_params=SMALL,
        name="prep",
    )(off_chip(rank), dangling)


def pack(wanted, source, slab, message, out_hbm, sem):
    peers = message.shape[0]
    seeds = source.shape[1]
    parts = sem.shape[0]
    per = peers // parts

    def send(c):
        span = pl.ds(c * per, per)
        return pltpu.make_async_copy(message.at[span], out_hbm.at[span], sem.at[c])

    def one(p, carry):
        for k in range(CAP):
            message[p, k * seeds : (k + 1) * seeds, :] = source[wanted[p, k]]
        message[p, CAP * seeds :, :] = slab
        return carry

    for c in range(parts):
        lax.fori_loop(c * per, (c + 1) * per, one, 0, unroll=8)
        send(c).start()
    for c in range(parts):
        send(c).wait()


def pack_kernel(wanted_ref, source_ref, slab_ref, out_hbm, message, sem):
    pack(wanted_ref, source_ref, slab_ref[...], message, out_hbm, sem)


def pack_first(wanted, source, slab, peers):
    _, seeds, width = source.shape
    shape = (peers, CAP * seeds + SLAB, width)
    return pl.pallas_call(
        pack_kernel,
        out_shape=in_hbm(shape, BF16),
        in_specs=[smem(), vmem(), vmem()],
        out_specs=hbm(),
        scratch_shapes=[VMEM(shape, BF16), pltpu.SemaphoreType.DMA((4,))],
        compiler_params=SMALL,
        name="pack",
    )(wanted, source, slab)


def band_kernel(source_hbm, tiles_hbm, out_hbm, source, tiles, banded, sem, source_sem, out_sem):
    blocks, seeds, width = banded.shape
    chunks = sem.shape[0]
    per = blocks // chunks

    def fetch(c):
        span = pl.ds(c * per, per)
        return pltpu.make_async_copy(tiles_hbm.at[span], tiles.at[span], sem.at[c])

    def flush(c):
        span = pl.ds(c * per, per)
        return pltpu.make_async_copy(banded.at[span], out_hbm.at[span], out_sem.at[c])

    own = pltpu.make_async_copy(source_hbm, source, source_sem)
    own.start()
    for c in range(chunks):
        fetch(c).start()
    zero = jnp.zeros((seeds, width), BF16)
    own.wait()
    for c in range(chunks):
        fetch(c).wait()
        for b in range(c * per, (c + 1) * per):
            before = source[b - 1] if b > 0 else zero
            after = source[b + 1] if b + 1 < blocks else zero
            x = jnp.concatenate([before, source[b], after], axis=1)
            w = jnp.concatenate([tiles[b, 0], tiles[b, 1], tiles[b, 2]], axis=1)
            banded[b] = dot_nt(x, w)
        flush(c).start()
    for c in range(chunks):
        flush(c).wait()


def band(source, tiles):
    return pl.pallas_call(
        band_kernel,
        out_shape=in_hbm(source.shape, F32),
        in_specs=[hbm(), hbm()],
        out_specs=hbm(),
        scratch_shapes=[
            VMEM(source.shape, BF16),
            VMEM(tiles.shape, BF16),
            VMEM(source.shape, F32),
            pltpu.SemaphoreType.DMA((8,)),
            pltpu.SemaphoreType.DMA,
            pltpu.SemaphoreType.DMA((8,)),
        ],
        compiler_params=MIDDLE,
        name="band",
    )(off_chip(source), off_chip(tiles))


UNROLL = 32
AHEAD = 6


def finish_kernel(last, vertices, *refs):
    (first_ref, count_ref, slot_ref, target_ref, wanted_ref) = refs[:5]
    (seed_ref, dangling_ref, left_ref, right_ref, fetched) = refs[5:10]
    banded_hbm, rank_hbm, tiles_hbm, band_hbm = refs[10:14]
    if last:
        next_hbm, stats_ref = refs[14:16]
        scratch = refs[16:]
    else:
        next_hbm, stats_ref, source_hbm, head_ref, tail_ref, message_hbm = refs[14:20]
        source, message, source_sem, send_sem = refs[20:24]
        scratch = refs[24:]
    tiles, acc, banded, rank, edges, edge_sem, tile_sem, load_sem, out_sem = scratch
    blocks, seeds, width = banded.shape
    parts = out_sem.shape[0]
    span = blocks // parts

    def edge_copy(k):
        at = band_hbm.at[0, 0] if k == 0 else band_hbm.at[blocks - 1, 2]
        return pltpu.make_async_copy(at, edges.at[k], edge_sem.at[k])

    def tile_copy(g):
        at = pl.ds(g * UNROLL, UNROLL)
        return pltpu.make_async_copy(tiles_hbm.at[at], tiles.at[at], tile_sem.at[g])

    def rank_store(c):
        cols = pl.ds(c * span * width, span * width)
        return pltpu.make_async_copy(rank.at[:, cols], next_hbm.at[:, cols], out_sem.at[c])

    def source_store(c):
        at = pl.ds(c * span, span)
        return pltpu.make_async_copy(source.at[at], source_hbm.at[at], source_sem.at[c])

    used = (count_ref[0] + UNROLL - 1) // UNROLL
    for k in range(2):
        edge_copy(k).start()
    for g in range(AHEAD):

        @pl.when(g < used)
        def _():
            tile_copy(g).start()

    mass_row = jnp.sum(jnp.sum(fetched[:, CAP * seeds :, :].astype(F32), axis=0), axis=0, keepdims=True)
    share = jnp.broadcast_to(to_column(mass_row, seeds) / vertices, (seeds, width))
    zero = jnp.zeros((seeds, width), BF16)
    acc[...] = jnp.zeros_like(acc)
    for k in range(2):
        edge_copy(k).wait()
    acc[0] = dot_nt(left_ref[...], edges[0])
    acc[blocks - 1] = acc[blocks - 1] + dot_nt(right_ref[...], edges[1])

    def operand(t):
        slot = slot_ref[0, t]
        at = pl.multiple_of((slot % CAP) * seeds, seeds)
        return fetched[slot // CAP, pl.ds(at, seeds), :]

    def group(g, carry):
        tile_copy(g).wait()

        @pl.when(g + AHEAD < used)
        def _():
            tile_copy(g + AHEAD).start()

        first = g * UNROLL
        products = []
        for u in range(0, UNROLL, 2):
            one, two = first + u, first + u + 1
            x = jnp.concatenate(
                [
                    jnp.concatenate([operand(one), zero], axis=1),
                    jnp.concatenate([zero, operand(two)], axis=1),
                ],
                axis=0,
            )
            y = dot_nt(x, jnp.concatenate([tiles[one], tiles[two]], axis=1))
            products += [y[:seeds], y[seeds:]]
        for u in range(UNROLL):
            row = target_ref[0, first + u]
            acc[row] = acc[row] + products[u]
        return carry

    early = jnp.minimum(used, 4)
    lax.fori_loop(0, early, group, 0)
    loads = (
        pltpu.make_async_copy(banded_hbm, banded, load_sem.at[0]),
        pltpu.make_async_copy(rank_hbm, rank, load_sem.at[1]),
    )
    for load in loads:
        load.start()
    lax.fori_loop(early, used, group, 0)
    for load in loads:
        load.wait()

    away = jnp.broadcast_to(seed_ref[...] - first_ref[0], (seeds, width)) - lax.broadcasted_iota(
        I32, (seeds, width), 1
    )

    def update(b, carry):
        gap, other = carry
        cols = pl.ds(pl.multiple_of(b * width, width), width)
        old = rank[:, cols]
        at_seed = away == b * width
        new = DAMP * (banded[b] + acc[b] + share) + jnp.where(at_seed, 1.0 - DAMP, 0.0)
        rank[:, cols] = new
        gap = gap + jnp.abs(new - old)
        if last:
            return gap, other + jnp.where(at_seed, new, 0.0)
        dead = jnp.broadcast_to(dangling_ref[pl.ds(b, 1), :], (seeds, width)) != 0
        kept = jnp.where(dead, 0.0, new)
        source[b] = kept.astype(BF16)
        return gap, other + (new - kept)

    carry = (jnp.zeros((seeds, width), F32), jnp.zeros((seeds, width), F32))
    for c in range(parts):
        carry = lax.fori_loop(c * span, (c + 1) * span, update, carry, unroll=8)
        rank_store(c).start()
        if not last:
            source_store(c).start()
    gap, other = carry
    if not last:
        pack(wanted_ref, source, mass_slab(other), message, message_hbm, send_sem)
        head_ref[...] = source[0]
        tail_ref[...] = source[blocks - 1]
        stats_ref[1:2, :] = jnp.zeros((1, 128), F32)
    else:
        stats_ref[1:2, :] = to_row(jnp.sum(other, axis=1, keepdims=True))
    stats_ref[0:1, :] = to_row(jnp.sum(gap, axis=1, keepdims=True))
    for c in range(parts):
        rank_store(c).wait()
        if not last:
            source_store(c).wait()


def finish(last, vertices, *operands):
    fetched, banded, rank, tiles = operands[9:13]
    operands = operands[:10] + tuple(off_chip(x) for x in operands[10:])
    blocks, seeds, width = banded.shape
    out_shape = [in_hbm(rank.shape, F32), shaped((2, 128), F32)]
    out_specs = [hbm(), vmem()]
    scratch = []
    if not last:
        edge = shaped((seeds, width), BF16)
        out_shape += [in_hbm((blocks, seeds, width), BF16), edge, edge, in_hbm(fetched.shape, BF16)]
        out_specs += [hbm(), vmem(), vmem(), hbm()]
        scratch = [
            VMEM((blocks, seeds, width), BF16),
            VMEM(fetched.shape, BF16),
            pltpu.SemaphoreType.DMA((8,)),
            pltpu.SemaphoreType.DMA((4,)),
        ]
    return pl.pallas_call(
        functools.partial(finish_kernel, last, vertices),
        out_shape=tuple(out_shape),
        in_specs=[smem()] * 5 + [vmem()] * 5 + [hbm()] * 4,
        out_specs=tuple(out_specs),
        scratch_shapes=scratch
        + [
            VMEM(tiles.shape, BF16),
            VMEM((blocks + 1, seeds, width), F32),
            VMEM((blocks, seeds, width), F32),
            VMEM(rank.shape, F32),
            VMEM((2, width, width), BF16),
            pltpu.SemaphoreType.DMA((2,)),
            pltpu.SemaphoreType.DMA((tiles.shape[0] // UNROLL,)),
            pltpu.SemaphoreType.DMA((2,)),
            pltpu.SemaphoreType.DMA((8,)),
        ],
        compiler_params=PARAMS,
        name="finish",
    )(*operands)


def stats_kernel(seeds, vertices, group_ref, got_ref, change_ref, total_ref, own_ref):
    got = got_ref[...]
    odd = lax.broadcasted_iota(I32, got.shape, 0) % 2 == 1
    one = jnp.sum(jnp.where(odd, got, 0.0), axis=0, keepdims=True)
    zero = jnp.sum(jnp.where(odd, 0.0, got), axis=0, keepdims=True)
    mine = jnp.where(group_ref[0] == 1, one, zero)
    both = one + zero
    for i in range(ITERS):
        lanes = slice(i * seeds, (i + 1) * seeds)
        change_ref[i : i + 1, :] = mine[:, lanes] / vertices
        total_ref[:, i : i + 1] = jnp.sum(both[:, lanes] / vertices, axis=1, keepdims=True) / (2 * seeds)
    own_ref[...] = mine[:, ITERS * seeds :]


def on_device(rank_in, band_tiles, off_tiles, tile_src, tile_row, tile_count, seed_ids, dangling):
    blocks, _, width, _ = band_tiles.shape
    seeds = rank_in.shape[0]
    peers = lax.axis_size("dom")
    groups = lax.axis_size("seed")
    vertices = blocks * width * peers
    first = (lax.axis_index("dom") * (blocks * width)).astype(I32).reshape(1)
    group = lax.axis_index("seed").astype(I32).reshape(1)
    dangling = dangling.reshape(blocks, width)
    seeds_at = seed_ids.reshape(seeds, 1)

    request, slot, target = plan(tile_count, tile_src, tile_row, peers, blocks)
    wanted = lax.all_to_all(request, "dom", split_axis=0, concat_axis=0, tiled=True)
    source, slab, head, tail = prep(rank_in, dangling, blocks)
    message = pack_first(wanted, source, slab, peers)
    rank = rank_in
    rows = []
    for iteration in range(ITERS):
        last = iteration + 1 == ITERS
        fetched = lax.all_to_all(message, "dom", split_axis=0, concat_axis=0, tiled=True)
        left = lax.ppermute(tail, "dom", [(i, i + 1) for i in range(peers - 1)])
        right = lax.ppermute(head, "dom", [(i + 1, i) for i in range(peers - 1)])
        banded = band(source, band_tiles)
        done = finish(
            last,
            vertices,
            first,
            tile_count,
            slot,
            target,
            wanted,
            seeds_at,
            dangling,
            left,
            right,
            fetched,
            banded,
            rank,
            off_tiles,
            band_tiles,
        )
        rank, stats = done[:2]
        rows.append(stats[0:1, :seeds])
        if not last:
            source, head, tail, message = done[2:]
    rows.append(stats[1:2, :seeds])
    line = jnp.concatenate(rows, axis=1)
    got = lax.all_to_all(
        jnp.broadcast_to(line, (peers * groups, line.shape[1])),
        ("dom", "seed"),
        split_axis=0,
        concat_axis=0,
        tiled=True,
    )
    change, total, own = pl.pallas_call(
        functools.partial(stats_kernel, seeds, vertices),
        out_shape=(shaped((ITERS, seeds), F32), shaped((1, ITERS), F32), shaped((1, seeds), F32)),
        in_specs=[smem(), vmem()],
        out_specs=(vmem(),) * 3,
        name="stats",
    )(group, got)
    return (rank, change, total.reshape(ITERS), own.reshape(seeds))


def solution(mesh):
    return jax.shard_map(
        on_device,
        mesh=mesh,
        in_specs=(
            P("seed", "dom"),
            P("dom", None, None, None),
            P("dom", None, None),
            P("dom", None),
            P("dom", None),
            P("dom"),
            P("seed"),
            P("dom"),
        ),
        out_specs=(P("seed", "dom"), P(None, "seed"), P(), P("seed")),
        check_vma=False,
    )
```

```python
import functools

import jax
import jax.numpy as jnp
from jax import lax
from jax.experimental import pallas as pl
from jax.experimental.pallas import tpu as pltpu
from jax.sharding import PartitionSpec as P

CAP = 2
ITERS = 3
DAMP = 0.85

BF16 = jnp.bfloat16
F32 = jnp.float32
I32 = jnp.int32
VMEM = pltpu.VMEM
NT = (((1,), (1,)), ((), ()))
SLAB = 8
PARAMS = pltpu.CompilerParams(vmem_limit_bytes=44 << 20)
MIDDLE = pltpu.CompilerParams(vmem_limit_bytes=34 << 20)
SMALL = pltpu.CompilerParams(vmem_limit_bytes=16 << 20)


def vmem():
    return pl.BlockSpec(memory_space=pltpu.VMEM)


def smem():
    return pl.BlockSpec(memory_space=pltpu.SMEM)


def hbm():
    return pl.BlockSpec(memory_space=pltpu.HBM)


def in_hbm(shape, dtype):
    return pltpu.HBM(shape, dtype)


def off_chip(x):
    return pltpu.with_memory_space_constraint(x, pltpu.HBM)


def shaped(shape, dtype):
    return jax.ShapeDtypeStruct(shape, dtype)


def dot_nt(x, w):
    return lax.dot_general(x, w, NT, preferred_element_type=F32)


def plan_kernel(peers, blocks, count_ref, src_ref, row_ref, request_ref, slot_ref, target_ref):
    slots = src_ref.shape[1]
    ids = src_ref[...]
    live = lax.broadcasted_iota(I32, (1, slots), 1) < count_ref[0]
    holder = ids // blocks
    inside = (ids - holder * blocks).astype(F32)
    peer = lax.broadcasted_iota(I32, (peers, slots), 0)
    held = jnp.broadcast_to(holder, (peers, slots)) == peer
    asked = jnp.logical_and(held, jnp.broadcast_to(live, (peers, slots)))
    block_of = jnp.broadcast_to(inside, (peers, slots))
    low = jnp.min(jnp.where(asked, block_of, float(blocks - 1)), axis=1, keepdims=True)
    high = jnp.max(jnp.where(asked, block_of, 0.0), axis=1, keepdims=True)
    lane = lax.broadcasted_iota(I32, request_ref.shape, 1)
    request_ref[...] = jnp.where(lane == 0, low, high).astype(I32)
    low_of = jnp.sum(jnp.where(held, low, 0.0), axis=0, keepdims=True)
    slot_ref[...] = holder * CAP + jnp.where(inside == low_of, 0, 1)
    target_ref[...] = jnp.where(live, row_ref[...], blocks)


def plan(tile_count, tile_src, tile_row, peers, blocks):
    slots = tile_src.shape[1]
    return pl.pallas_call(
        functools.partial(plan_kernel, peers, blocks),
        out_shape=(shaped((peers, 128), I32), shaped((1, slots), I32), shaped((1, slots), I32)),
        in_specs=[smem(), vmem(), vmem()],
        out_specs=(vmem(), vmem(), vmem()),
        name="plan",
    )(tile_count, tile_src, tile_row)


def eye(rows, start=0):
    lane = lax.broadcasted_iota(I32, (rows, 128), 1)
    return lax.broadcasted_iota(I32, (rows, 128), 0) + start == lane


def to_row(column, start=0):
    return jnp.sum(jnp.where(eye(column.shape[0], start), column, 0.0), axis=0, keepdims=True)


def to_column(row, seeds):
    return jnp.sum(jnp.where(eye(seeds), row, 0.0), axis=1, keepdims=True)


def mass_slab(mass):
    row = to_row(jnp.sum(mass, axis=1, keepdims=True))
    high = row.astype(BF16).astype(F32)
    rest = row - high
    middle = rest.astype(BF16).astype(F32)
    low = rest - middle
    at = lax.broadcasted_iota(I32, (SLAB, 128), 0)
    slab = jnp.where(at == 0, high, jnp.where(at == 1, middle, jnp.where(at == 2, low, 0.0)))
    return slab.astype(BF16)


def prep_kernel(rank_hbm, dangling_ref, source_ref, slab_ref, head_ref, tail_ref, rank, sem):
    blocks, seeds, width = source_ref.shape
    chunks = sem.shape[0]
    per = blocks // chunks

    def fetch(c):
        cols = pl.ds(c * per * width, per * width)
        return pltpu.make_async_copy(rank_hbm.at[:, cols], rank.at[:, cols], sem.at[c])

    for c in range(chunks):
        fetch(c).start()
    mass = jnp.zeros((seeds, width), F32)
    for c in range(chunks):
        fetch(c).wait()
        for b in range(c * per, (c + 1) * per):
            old = rank[:, b * width : (b + 1) * width]
            dead = jnp.broadcast_to(dangling_ref[b : b + 1, :], (seeds, width)) != 0
            kept = jnp.where(dead, 0.0, old)
            mass += old - kept
            source_ref[b] = kept.astype(BF16)
    slab_ref[...] = mass_slab(mass)
    head_ref[...] = source_ref[0]
    tail_ref[...] = source_ref[blocks - 1]


def prep(rank, dangling, blocks):
    seeds = rank.shape[0]
    width = rank.shape[1] // blocks
    edge = shaped((seeds, width), BF16)
    return pl.pallas_call(
        prep_kernel,
        out_shape=(shaped((blocks, seeds, width), BF16), shaped((SLAB, 128), BF16), edge, edge),
        in_specs=[hbm(), vmem()],
        out_specs=(vmem(),) * 4,
        scratch_shapes=[VMEM(rank.shape, F32), pltpu.SemaphoreType.DMA((8,))],
        compiler_params=SMALL,
        name="prep",
    )(off_chip(rank), dangling)


def pack(wanted, source, slab, message, out_hbm, sem):
    peers = message.shape[0]
    seeds = source.shape[1]
    parts = sem.shape[0]
    per = peers // parts

    def send(c):
        span = pl.ds(c * per, per)
        return pltpu.make_async_copy(message.at[span], out_hbm.at[span], sem.at[c])

    def one(p, carry):
        for k in range(CAP):
            message[p, k * seeds : (k + 1) * seeds, :] = source[wanted[p, k]]
        message[p, CAP * seeds :, :] = slab
        return carry

    for c in range(parts):
        lax.fori_loop(c * per, (c + 1) * per, one, 0, unroll=8)
        send(c).start()
    for c in range(parts):
        send(c).wait()


def pack_kernel(wanted_ref, source_ref, slab_ref, out_hbm, message, sem):
    pack(wanted_ref, source_ref, slab_ref[...], message, out_hbm, sem)


def pack_first(wanted, source, slab, peers):
    _, seeds, width = source.shape
    shape = (peers, CAP * seeds + SLAB, width)
    return pl.pallas_call(
        pack_kernel,
        out_shape=in_hbm(shape, BF16),
        in_specs=[smem(), vmem(), vmem()],
        out_specs=hbm(),
        scratch_shapes=[VMEM(shape, BF16), pltpu.SemaphoreType.DMA((4,))],
        compiler_params=SMALL,
        name="pack",
    )(wanted, source, slab)


def band_kernel(gap_at, rank_hbm, *refs):
    refs = list(refs)
    old_hbm = None if gap_at is None else refs.pop(0)
    tiles_hbm, dangling_ref, out_hbm = refs[:3]
    refs = refs[3:]
    gap_ref = None if gap_at is None else refs.pop(0)
    rank, source, tiles, banded, sem, rank_sem, out_sem = refs[:7]
    blocks, seeds, width = banded.shape
    chunks = sem.shape[0]
    per = blocks // chunks

    def fetch(c):
        span = pl.ds(c * per, per)
        return pltpu.make_async_copy(tiles_hbm.at[span], tiles.at[span], sem.at[c])

    def flush(c):
        span = pl.ds(c * per, per)
        return pltpu.make_async_copy(banded.at[span], out_hbm.at[span], out_sem.at[c])

    def fetch_rank(c):
        cols = pl.ds(c * per * width, per * width)
        return pltpu.make_async_copy(rank_hbm.at[:, cols], rank.at[:, cols], rank_sem.at[c])

    def fetch_old(c):
        cols = pl.ds(c * per * width, per * width)
        return pltpu.make_async_copy(old_hbm.at[:, cols], refs[7].at[:, cols], refs[8].at[c])

    for c in range(chunks):
        fetch_rank(c).start()
        if gap_at is not None:
            fetch_old(c).start()
        fetch(c).start()

    gap = jnp.zeros((seeds, width), F32)

    def prepare(c, gap):
        fetch_rank(c).wait()
        if gap_at is not None:
            fetch_old(c).wait()
        for b in range(c * per, (c + 1) * per):
            cols = slice(b * width, (b + 1) * width)
            new = rank[:, cols]
            dead = jnp.broadcast_to(dangling_ref[b : b + 1, :], (seeds, width)) != 0
            source[b] = jnp.where(dead, 0.0, new).astype(BF16)
            if gap_at is not None:
                gap = gap + jnp.abs(new - refs[7][:, cols])
        return gap

    gap = prepare(0, gap)
    zero = jnp.zeros((seeds, width), BF16)
    for c in range(chunks):
        if c + 1 < chunks:
            gap = prepare(c + 1, gap)
        fetch(c).wait()
        for b in range(c * per, (c + 1) * per):
            before = source[b - 1] if b > 0 else zero
            after = source[b + 1] if b + 1 < blocks else zero
            x = jnp.concatenate([before, source[b], after], axis=1)
            w = jnp.concatenate([tiles[b, 0], tiles[b, 1], tiles[b, 2]], axis=1)
            banded[b] = dot_nt(x, w)
        flush(c).start()
    if gap_at is not None:
        gap_ref[...] = to_row(jnp.sum(gap, axis=1, keepdims=True), gap_at)
    for c in range(chunks):
        flush(c).wait()


def band(gap_at, rank, old, tiles, dangling):
    blocks, _, width, _ = tiles.shape
    seeds = rank.shape[0]
    shape = (blocks, seeds, width)
    ranks = [rank] if gap_at is None else [rank, old]
    out_shape = [in_hbm(shape, F32)]
    out_specs = [hbm()]
    extra = []
    if gap_at is not None:
        out_shape.append(shaped((1, 128), F32))
        out_specs.append(vmem())
        extra = [VMEM(rank.shape, F32), pltpu.SemaphoreType.DMA((8,))]
    return pl.pallas_call(
        functools.partial(band_kernel, gap_at),
        out_shape=tuple(out_shape),
        in_specs=[hbm()] * (len(ranks) + 1) + [vmem()],
        out_specs=tuple(out_specs),
        scratch_shapes=[
            VMEM(rank.shape, F32),
            VMEM(shape, BF16),
            VMEM(tiles.shape, BF16),
            VMEM(shape, F32),
            pltpu.SemaphoreType.DMA((8,)),
            pltpu.SemaphoreType.DMA((8,)),
            pltpu.SemaphoreType.DMA((8,)),
        ]
        + extra,
        compiler_params=MIDDLE,
        name="band",
    )(*(off_chip(x) for x in ranks), off_chip(tiles), dangling)


UNROLL = 64
PIECE = 32
AHEAD = 6
DEPTH = 8


def finish_kernel(last, vertices, *refs):
    (first_ref, count_ref, slot_ref, target_ref, wanted_ref) = refs[:5]
    (seed_ref, dangling_ref, left_ref, right_ref, fetched) = refs[5:10]
    banded_hbm, tiles_hbm, band_hbm = refs[10:13]
    if last:
        rank_hbm, gap_one_ref, gap_two_ref, next_hbm, line_ref, rank_sem = refs[13:19]
        scratch = refs[19:]
    else:
        next_hbm, head_ref, tail_ref, message_hbm, source, message, send_sem = refs[13:20]
        scratch = refs[20:]
    tiles, acc, banded, rank, edges, edge_sem, tile_sem, base_sem, out_sem = scratch
    blocks, seeds, width = banded.shape
    parts = out_sem.shape[0]
    span = blocks // parts

    def edge_copy(k):
        at = band_hbm.at[0, 0] if k == 0 else band_hbm.at[blocks - 1, 2]
        return pltpu.make_async_copy(at, edges.at[k], edge_sem.at[k])

    def tile_copy(g):
        at = pl.ds(g * PIECE, PIECE)
        return pltpu.make_async_copy(tiles_hbm.at[at], tiles.at[at], tile_sem.at[g])

    def rank_store(c):
        cols = pl.ds(c * span * width, span * width)
        return pltpu.make_async_copy(rank.at[:, cols], next_hbm.at[:, cols], out_sem.at[c])

    trips = (count_ref[0] + UNROLL - 1) // UNROLL
    pieces = trips * (UNROLL // PIECE)
    for g in range(AHEAD):

        @pl.when(g < pieces)
        def _():
            tile_copy(g).start()

    mass_row = jnp.sum(jnp.sum(fetched[:, CAP * seeds :, :].astype(F32), axis=0), axis=0, keepdims=True)
    share = jnp.broadcast_to(to_column(mass_row, seeds) / vertices, (seeds, width))
    zero = jnp.zeros((seeds, width), BF16)
    acc[...] = jnp.zeros_like(acc)

    def operand(t):
        slot = slot_ref[0, t]
        at = pl.multiple_of((slot % CAP) * seeds, seeds)
        return fetched[slot // CAP, pl.ds(at, seeds), :]

    def group(g, carry):
        for k in range(UNROLL // PIECE):
            piece = g * (UNROLL // PIECE) + k
            tile_copy(piece).wait()

            @pl.when(piece + AHEAD < pieces)
            def _():
                tile_copy(piece + AHEAD).start()

        first = g * UNROLL
        waiting = []

        def add(most):
            while len(waiting) > most:
                t, y = waiting.pop(0)
                for k in range(2):
                    row = target_ref[0, t + k]
                    acc[row] = acc[row] + y[k * seeds : (k + 1) * seeds]

        for u in range(0, UNROLL, 2):
            one, two = first + u, first + u + 1
            x = jnp.concatenate(
                [
                    jnp.concatenate([operand(one), zero], axis=1),
                    jnp.concatenate([zero, operand(two)], axis=1),
                ],
                axis=0,
            )
            waiting.append((one, dot_nt(x, jnp.concatenate([tiles[one], tiles[two]], axis=1))))
            add(DEPTH)
        add(0)
        return carry

    early = jnp.minimum(trips, 2)
    lax.fori_loop(0, early, group, 0)
    loads = [pltpu.make_async_copy(banded_hbm, banded, base_sem)]
    if last:
        loads.append(pltpu.make_async_copy(rank_hbm, rank, rank_sem))
    for load in loads:
        load.start()
    for k in range(2):
        edge_copy(k).start()
    lax.fori_loop(early, trips, group, 0)
    for k in range(2):
        edge_copy(k).wait()
    acc[0] = acc[0] + dot_nt(left_ref[...], edges[0])
    acc[blocks - 1] = acc[blocks - 1] + dot_nt(right_ref[...], edges[1])
    for load in loads:
        load.wait()

    away = jnp.broadcast_to(seed_ref[...] - first_ref[0], (seeds, width)) - lax.broadcasted_iota(
        I32, (seeds, width), 1
    )

    def update(b, carry):
        cols = pl.ds(pl.multiple_of(b * width, width), width)
        at_seed = away == b * width
        new = DAMP * (banded[b] + acc[b] + share) + jnp.where(at_seed, 1.0 - DAMP, 0.0)
        if last:
            gap, own = carry
            gap = gap + jnp.abs(new - rank[:, cols])
            rank[:, cols] = new
            return gap, own + jnp.where(at_seed, new, 0.0)
        rank[:, cols] = new
        dead = jnp.broadcast_to(dangling_ref[pl.ds(b, 1), :], (seeds, width)) != 0
        kept = jnp.where(dead, 0.0, new)
        source[b] = kept.astype(BF16)
        return carry + (new - kept)

    nothing = jnp.zeros((seeds, width), F32)
    carry = (nothing, nothing) if last else nothing
    for c in range(parts):
        carry = lax.fori_loop(c * span, (c + 1) * span, update, carry, unroll=8)
        rank_store(c).start()
    if last:
        gap, own = (jnp.sum(x, axis=1, keepdims=True) for x in carry)
        line = jnp.concatenate(
            [gap_one_ref[...] + gap_two_ref[...], to_row(gap) + to_row(own, seeds)], axis=1
        )
        line_ref[...] = jnp.broadcast_to(line[:, None, :], line_ref.shape)
    else:
        pack(wanted_ref, source, mass_slab(carry), message, message_hbm, send_sem)
        head_ref[...] = source[0]
        tail_ref[...] = source[blocks - 1]
    for c in range(parts):
        rank_store(c).wait()


def finish(last, vertices, devices, scalars, vectors, arrays, old=(), gaps=()):
    fetched = vectors[-1]
    banded, tiles, _ = arrays
    blocks, seeds, width = banded.shape
    shape = (seeds, blocks * width)
    operands = tuple(scalars) + tuple(vectors) + tuple(off_chip(x) for x in tuple(arrays) + tuple(old)) + tuple(gaps)
    if last:
        out_shape = (in_hbm(shape, F32), shaped((devices, 1, 256), F32))
        out_specs = (hbm(), vmem())
        scratch = [pltpu.SemaphoreType.DMA]
    else:
        edge = shaped((seeds, width), BF16)
        out_shape = (in_hbm(shape, F32), edge, edge, in_hbm(fetched.shape, BF16))
        out_specs = (hbm(), vmem(), vmem(), hbm())
        scratch = [
            VMEM((blocks, seeds, width), BF16),
            VMEM(fetched.shape, BF16),
            pltpu.SemaphoreType.DMA((4,)),
        ]
    return pl.pallas_call(
        functools.partial(finish_kernel, last, vertices),
        out_shape=out_shape,
        in_specs=[smem()] * len(scalars)
        + [vmem()] * len(vectors)
        + [hbm()] * (len(arrays) + len(old))
        + [vmem()] * len(gaps),
        out_specs=out_specs,
        scratch_shapes=scratch
        + [
            VMEM(tiles.shape, BF16),
            VMEM((blocks + 1, seeds, width), F32),
            VMEM((blocks, seeds, width), F32),
            VMEM(shape, F32),
            VMEM((2, width, width), BF16),
            pltpu.SemaphoreType.DMA((2,)),
            pltpu.SemaphoreType.DMA((tiles.shape[0] // PIECE,)),
            pltpu.SemaphoreType.DMA,
            pltpu.SemaphoreType.DMA((8,)),
        ],
        compiler_params=PARAMS,
        name="finish",
    )(*operands)


def stats_kernel(seeds, vertices, group_ref, got_ref, change_ref, total_ref, own_ref):
    devices, _, lanes = got_ref.shape
    sums = [jnp.zeros((1, lanes), F32), jnp.zeros((1, lanes), F32)]
    for d in range(devices):
        sums[d % 2] = sums[d % 2] + got_ref[d]
    mine = jnp.where(group_ref[0] == 1, sums[1], sums[0])
    both = sums[0] + sums[1]
    for i in range(ITERS):
        at = slice(i * seeds, (i + 1) * seeds)
        change_ref[i : i + 1, :] = mine[:, at] / vertices
        total_ref[:, i : i + 1] = jnp.sum(both[:, at] / vertices, axis=1, keepdims=True) / (2 * seeds)
    own_ref[...] = mine[:, ITERS * seeds :]


def on_device(rank_in, band_tiles, off_tiles, tile_src, tile_row, tile_count, seed_ids, dangling):
    blocks, _, width, _ = band_tiles.shape
    seeds = rank_in.shape[0]
    peers = lax.axis_size("dom")
    devices = peers * lax.axis_size("seed")
    vertices = blocks * width * peers
    first = (lax.axis_index("dom") * (blocks * width)).astype(I32).reshape(1)
    group = lax.axis_index("seed").astype(I32).reshape(1)
    dangling = dangling.reshape(blocks, width)
    seeds_at = seed_ids.reshape(seeds, 1)

    request, slot, target = plan(tile_count, tile_src, tile_row, peers, blocks)
    wanted = lax.all_to_all(request, "dom", split_axis=0, concat_axis=0, tiled=True)
    source, slab, head, tail = prep(rank_in, dangling, blocks)
    message = pack_first(wanted, source, slab, peers)
    old, rank = None, rank_in
    gaps = []
    for iteration in range(ITERS):
        last = iteration + 1 == ITERS
        fetched = lax.all_to_all(message, "dom", split_axis=0, concat_axis=0, tiled=True)
        left = lax.ppermute(tail, "dom", [(i, i + 1) for i in range(peers - 1)])
        right = lax.ppermute(head, "dom", [(i + 1, i) for i in range(peers - 1)])
        gap_at = (iteration - 1) * seeds if iteration > 0 else None
        banded, *gap = band(gap_at, rank, old, band_tiles, dangling)
        gaps += gap
        scalars = (first, tile_count, slot, target, wanted)
        vectors = (seeds_at, dangling, left, right, fetched)
        arrays = (banded, off_tiles, band_tiles)
        if last:
            rank, line = finish(last, vertices, devices, scalars, vectors, arrays, (rank,), gaps)
        else:
            old = rank
            rank, head, tail, message = finish(last, vertices, devices, scalars, vectors, arrays)
    got = lax.all_to_all(line, ("dom", "seed"), split_axis=0, concat_axis=0, tiled=True)
    change, total, own = pl.pallas_call(
        functools.partial(stats_kernel, seeds, vertices),
        out_shape=(shaped((ITERS, seeds), F32), shaped((1, ITERS), F32), shaped((1, seeds), F32)),
        in_specs=[smem(), vmem()],
        out_specs=(vmem(),) * 3,
        name="stats",
    )(group, got)
    return (rank, change, total.reshape(ITERS), own.reshape(seeds))


def solution(mesh):
    return jax.shard_map(
        on_device,
        mesh=mesh,
        in_specs=(
            P("seed", "dom"),
            P("dom", None, None, None),
            P("dom", None, None),
            P("dom", None),
            P("dom", None),
            P("dom"),
            P("seed"),
            P("dom"),
        ),
        out_specs=(P("seed", "dom"), P(None, "seed"), P(), P("seed")),
        check_vma=False,
    )
```

```python
import functools

import jax
import jax.numpy as jnp
from jax import lax
from jax.experimental import pallas as pl
from jax.experimental.pallas import tpu as pltpu
from jax.sharding import PartitionSpec as P

CAP = 2
ITERS = 3
DAMP = 0.85

BF16 = jnp.bfloat16
F32 = jnp.float32
I32 = jnp.int32
VMEM = pltpu.VMEM
NT = (((1,), (1,)), ((), ()))
SLAB = 8
PARAMS = pltpu.CompilerParams(vmem_limit_bytes=44 << 20)
MIDDLE = pltpu.CompilerParams(vmem_limit_bytes=34 << 20)
SMALL = pltpu.CompilerParams(vmem_limit_bytes=16 << 20)


def vmem():
    return pl.BlockSpec(memory_space=pltpu.VMEM)


def smem():
    return pl.BlockSpec(memory_space=pltpu.SMEM)


def hbm():
    return pl.BlockSpec(memory_space=pltpu.HBM)


def in_hbm(shape, dtype):
    return pltpu.HBM(shape, dtype)


def off_chip(x):
    return pltpu.with_memory_space_constraint(x, pltpu.HBM)


def shaped(shape, dtype):
    return jax.ShapeDtypeStruct(shape, dtype)


def dot_nt(x, w):
    return lax.dot_general(x, w, NT, preferred_element_type=F32)


def plan_kernel(peers, blocks, count_ref, src_ref, row_ref, request_ref, slot_ref, target_ref):
    slots = src_ref.shape[1]
    ids = src_ref[...]
    live = lax.broadcasted_iota(I32, (1, slots), 1) < count_ref[0]
    holder = ids // blocks
    inside = (ids - holder * blocks).astype(F32)
    peer = lax.broadcasted_iota(I32, (peers, slots), 0)
    held = jnp.broadcast_to(holder, (peers, slots)) == peer
    asked = jnp.logical_and(held, jnp.broadcast_to(live, (peers, slots)))
    block_of = jnp.broadcast_to(inside, (peers, slots))
    low = jnp.min(jnp.where(asked, block_of, float(blocks - 1)), axis=1, keepdims=True)
    high = jnp.max(jnp.where(asked, block_of, 0.0), axis=1, keepdims=True)
    lane = lax.broadcasted_iota(I32, request_ref.shape, 1)
    request_ref[...] = jnp.where(lane == 0, low, high).astype(I32)
    low_of = jnp.sum(jnp.where(held, low, 0.0), axis=0, keepdims=True)
    slot_ref[...] = holder * CAP + jnp.where(inside == low_of, 0, 1)
    target_ref[...] = jnp.where(live, row_ref[...], blocks)


def plan(tile_count, tile_src, tile_row, peers, blocks):
    slots = tile_src.shape[1]
    return pl.pallas_call(
        functools.partial(plan_kernel, peers, blocks),
        out_shape=(shaped((peers, 128), I32), shaped((1, slots), I32), shaped((1, slots), I32)),
        in_specs=[smem(), vmem(), vmem()],
        out_specs=(vmem(), vmem(), vmem()),
        name="plan",
    )(tile_count, tile_src, tile_row)


def eye(rows, start=0):
    lane = lax.broadcasted_iota(I32, (rows, 128), 1)
    return lax.broadcasted_iota(I32, (rows, 128), 0) + start == lane


def to_row(column, start=0):
    return jnp.sum(jnp.where(eye(column.shape[0], start), column, 0.0), axis=0, keepdims=True)


def to_column(row, seeds):
    return jnp.sum(jnp.where(eye(seeds), row, 0.0), axis=1, keepdims=True)


def mass_slab(mass):
    row = to_row(jnp.sum(mass, axis=1, keepdims=True))
    high = row.astype(BF16).astype(F32)
    rest = row - high
    middle = rest.astype(BF16).astype(F32)
    low = rest - middle
    at = lax.broadcasted_iota(I32, (SLAB, 128), 0)
    slab = jnp.where(at == 0, high, jnp.where(at == 1, middle, jnp.where(at == 2, low, 0.0)))
    return slab.astype(BF16)


def prep_kernel(rank_hbm, dangling_ref, source_ref, slab_ref, head_ref, tail_ref, rank, sem):
    blocks, seeds, width = source_ref.shape
    chunks = sem.shape[0]
    per = blocks // chunks

    def fetch(c):
        cols = pl.ds(c * per * width, per * width)
        return pltpu.make_async_copy(rank_hbm.at[:, cols], rank.at[:, cols], sem.at[c])

    for c in range(chunks):
        fetch(c).start()
    mass = jnp.zeros((seeds, width), F32)
    for c in range(chunks):
        fetch(c).wait()
        for b in range(c * per, (c + 1) * per):
            old = rank[:, b * width : (b + 1) * width]
            dead = jnp.broadcast_to(dangling_ref[b : b + 1, :], (seeds, width)) != 0
            kept = jnp.where(dead, 0.0, old)
            mass += old - kept
            source_ref[b] = kept.astype(BF16)
    slab_ref[...] = mass_slab(mass)
    head_ref[...] = source_ref[0]
    tail_ref[...] = source_ref[blocks - 1]


def prep(rank, dangling, blocks):
    seeds = rank.shape[0]
    width = rank.shape[1] // blocks
    edge = shaped((seeds, width), BF16)
    return pl.pallas_call(
        prep_kernel,
        out_shape=(shaped((blocks, seeds, width), BF16), shaped((SLAB, 128), BF16), edge, edge),
        in_specs=[hbm(), vmem()],
        out_specs=(vmem(),) * 4,
        scratch_shapes=[VMEM(rank.shape, F32), pltpu.SemaphoreType.DMA((8,))],
        compiler_params=SMALL,
        name="prep",
    )(off_chip(rank), dangling)


def pack(wanted, source, slab, message, out_hbm, sem):
    peers = message.shape[0]
    seeds = source.shape[1]
    parts = sem.shape[0]
    per = peers // parts

    def send(c):
        span = pl.ds(c * per, per)
        return pltpu.make_async_copy(message.at[span], out_hbm.at[span], sem.at[c])

    def one(p, carry):
        for k in range(CAP):
            message[p, k * seeds : (k + 1) * seeds, :] = source[wanted[p, k]]
        message[p, CAP * seeds :, :] = slab
        return carry

    for c in range(parts):
        lax.fori_loop(c * per, (c + 1) * per, one, 0, unroll=8)
        send(c).start()
    for c in range(parts):
        send(c).wait()


def pack_kernel(wanted_ref, source_ref, slab_ref, out_hbm, message, sem):
    pack(wanted_ref, source_ref, slab_ref[...], message, out_hbm, sem)


def pack_first(wanted, source, slab, peers):
    _, seeds, width = source.shape
    shape = (peers, CAP * seeds + SLAB, width)
    return pl.pallas_call(
        pack_kernel,
        out_shape=in_hbm(shape, BF16),
        in_specs=[smem(), vmem(), vmem()],
        out_specs=hbm(),
        scratch_shapes=[VMEM(shape, BF16), pltpu.SemaphoreType.DMA((4,))],
        compiler_params=SMALL,
        name="pack",
    )(wanted, source, slab)


def from_seed(seed_ref, first_ref, width):
    seeds = seed_ref.shape[0]
    here = jnp.broadcast_to(seed_ref[...] - first_ref[0], (seeds, width))
    return here - lax.broadcasted_iota(I32, (seeds, width), 1)


def band_kernel(gap_at, first_ref, rank_hbm, *refs):
    refs = list(refs)
    old_hbm = None if gap_at is None else refs.pop(0)
    tiles_hbm, dangling_ref, seed_ref, out_hbm = refs[:4]
    refs = refs[4:]
    gap_ref = None if gap_at is None else refs.pop(0)
    rank, source, tiles, banded, sem, rank_sem, out_sem = refs[:7]
    blocks, seeds, width = banded.shape
    chunks = sem.shape[0]
    per = blocks // chunks

    def fetch(c):
        span = pl.ds(c * per, per)
        return pltpu.make_async_copy(tiles_hbm.at[span], tiles.at[span], sem.at[c])

    def flush(c):
        span = pl.ds(c * per, per)
        return pltpu.make_async_copy(banded.at[span], out_hbm.at[span], out_sem.at[c])

    def fetch_rank(c):
        cols = pl.ds(c * per * width, per * width)
        return pltpu.make_async_copy(rank_hbm.at[:, cols], rank.at[:, cols], rank_sem.at[c])

    def fetch_old(c):
        cols = pl.ds(c * per * width, per * width)
        return pltpu.make_async_copy(old_hbm.at[:, cols], refs[7].at[:, cols], refs[8].at[c])

    for c in range(chunks):
        fetch_rank(c).start()
        if gap_at is not None:
            fetch_old(c).start()
        fetch(c).start()

    gap = jnp.zeros((seeds, width), F32)

    def prepare(c, gap):
        fetch_rank(c).wait()
        if gap_at is not None:
            fetch_old(c).wait()
        for b in range(c * per, (c + 1) * per):
            cols = slice(b * width, (b + 1) * width)
            new = rank[:, cols]
            dead = jnp.broadcast_to(dangling_ref[b : b + 1, :], (seeds, width)) != 0
            source[b] = jnp.where(dead, 0.0, new).astype(BF16)
            if gap_at is not None:
                gap = gap + jnp.abs(new - refs[7][:, cols])
        return gap

    gap = prepare(0, gap)
    away = from_seed(seed_ref, first_ref, width)
    zero = jnp.zeros((seeds, width), BF16)
    for c in range(chunks):
        if c + 1 < chunks:
            gap = prepare(c + 1, gap)
        fetch(c).wait()
        for b in range(c * per, (c + 1) * per):
            before = source[b - 1] if b > 0 else zero
            after = source[b + 1] if b + 1 < blocks else zero
            x = jnp.concatenate([before, source[b], after], axis=1)
            w = jnp.concatenate([tiles[b, 0], tiles[b, 1], tiles[b, 2]], axis=1)
            banded[b] = DAMP * dot_nt(x, w) + jnp.where(away == b * width, 1.0 - DAMP, 0.0)
        flush(c).start()
    if gap_at is not None:
        gap_ref[...] = to_row(jnp.sum(gap, axis=1, keepdims=True), gap_at)
    for c in range(chunks):
        flush(c).wait()


def band(gap_at, first, rank, old, tiles, dangling, seeds_at):
    blocks, _, width, _ = tiles.shape
    seeds = rank.shape[0]
    shape = (blocks, seeds, width)
    ranks = [rank] if gap_at is None else [rank, old]
    out_shape = [in_hbm(shape, F32)]
    out_specs = [hbm()]
    extra = []
    if gap_at is not None:
        out_shape.append(shaped((1, 128), F32))
        out_specs.append(vmem())
        extra = [VMEM(rank.shape, F32), pltpu.SemaphoreType.DMA((8,))]
    return pl.pallas_call(
        functools.partial(band_kernel, gap_at),
        out_shape=tuple(out_shape),
        in_specs=[smem()] + [hbm()] * (len(ranks) + 1) + [vmem()] * 2,
        out_specs=tuple(out_specs),
        scratch_shapes=[
            VMEM(rank.shape, F32),
            VMEM(shape, BF16),
            VMEM(tiles.shape, BF16),
            VMEM(shape, F32),
            pltpu.SemaphoreType.DMA((8,)),
            pltpu.SemaphoreType.DMA((8,)),
            pltpu.SemaphoreType.DMA((8,)),
        ]
        + extra,
        compiler_params=MIDDLE,
        name="band",
    )(first, *(off_chip(x) for x in ranks), off_chip(tiles), dangling, seeds_at)


UNROLL = 64
DEPTH = 8


def finish_kernel(last, vertices, *refs):
    (first_ref, count_ref, slot_ref, target_ref, wanted_ref) = refs[:5]
    (seed_ref, dangling_ref, left_ref, right_ref, fetched) = refs[5:10]
    banded_hbm, tiles_hbm, band_hbm = refs[10:13]
    if last:
        rank_hbm, gap_one_ref, gap_two_ref, next_hbm, line_ref, rank_sem = refs[13:19]
        scratch = refs[19:]
    else:
        next_hbm, head_ref, tail_ref, message_hbm, source, message, send_sem = refs[13:20]
        scratch = refs[20:]
    tiles, acc, banded, rank, edges, edge_sem, tile_sem, base_sem, out_sem = scratch
    blocks, seeds, width = banded.shape
    parts = out_sem.shape[0]
    span = blocks // parts

    def edge_copy(k):
        at = band_hbm.at[0, 0] if k == 0 else band_hbm.at[blocks - 1, 2]
        return pltpu.make_async_copy(at, edges.at[k], edge_sem.at[k])

    def tile_copy(g):
        at = pl.ds(g * UNROLL, UNROLL)
        return pltpu.make_async_copy(tiles_hbm.at[at], tiles.at[at], tile_sem.at[g])

    def rank_store(c):
        cols = pl.ds(c * span * width, span * width)
        return pltpu.make_async_copy(rank.at[:, cols], next_hbm.at[:, cols], out_sem.at[c])

    trips = (count_ref[0] + UNROLL - 1) // UNROLL
    for g in range(tile_sem.shape[0]):

        @pl.when(g < trips)
        def _():
            tile_copy(g).start()

    loads = [pltpu.make_async_copy(banded_hbm, banded, base_sem)]
    if last:
        loads.append(pltpu.make_async_copy(rank_hbm, rank, rank_sem))
    for load in loads:
        load.start()
    for k in range(2):
        edge_copy(k).start()
    mass_row = jnp.sum(jnp.sum(fetched[:, CAP * seeds :, :].astype(F32), axis=0), axis=0, keepdims=True)
    share = jnp.broadcast_to(DAMP * (to_column(mass_row, seeds) / vertices), (seeds, width))
    zero = jnp.zeros((seeds, width), BF16)
    acc[...] = jnp.zeros_like(acc)

    def operand(t):
        slot = slot_ref[0, t]
        at = pl.multiple_of((slot % CAP) * seeds, seeds)
        return fetched[slot // CAP, pl.ds(at, seeds), :]

    def group(g, carry):
        tile_copy(g).wait()
        first = g * UNROLL
        waiting = []

        def add(most):
            while len(waiting) > most:
                t, y = waiting.pop(0)
                for k in range(2):
                    row = target_ref[0, t + k]
                    acc[row] = acc[row] + y[k * seeds : (k + 1) * seeds]

        for u in range(0, UNROLL, 2):
            one, two = first + u, first + u + 1
            x = jnp.concatenate(
                [
                    jnp.concatenate([operand(one), zero], axis=1),
                    jnp.concatenate([zero, operand(two)], axis=1),
                ],
                axis=0,
            )
            waiting.append((one, dot_nt(x, jnp.concatenate([tiles[one], tiles[two]], axis=1))))
            add(DEPTH)
        add(0)
        return carry

    lax.fori_loop(0, trips, group, 0)
    for k in range(2):
        edge_copy(k).wait()
    acc[0] = acc[0] + dot_nt(left_ref[...], edges[0])
    acc[blocks - 1] = acc[blocks - 1] + dot_nt(right_ref[...], edges[1])
    for load in loads:
        load.wait()

    if last:
        away = from_seed(seed_ref, first_ref, width)

    def update(b, carry):
        cols = pl.ds(pl.multiple_of(b * width, width), width)
        new = banded[b] + (DAMP * acc[b] + share)
        if last:
            gap, own = carry
            gap = gap + jnp.abs(new - rank[:, cols])
            rank[:, cols] = new
            return gap, own + jnp.where(away == b * width, new, 0.0)
        rank[:, cols] = new
        dead = jnp.broadcast_to(dangling_ref[pl.ds(b, 1), :], (seeds, width)) != 0
        kept = jnp.where(dead, 0.0, new)
        source[b] = kept.astype(BF16)
        return carry + (new - kept)

    nothing = jnp.zeros((seeds, width), F32)
    carry = (nothing, nothing) if last else nothing
    for c in range(parts):
        carry = lax.fori_loop(c * span, (c + 1) * span, update, carry, unroll=8)
        rank_store(c).start()
    if last:
        gap, own = (jnp.sum(x, axis=1, keepdims=True) for x in carry)
        line = jnp.concatenate(
            [gap_one_ref[...] + gap_two_ref[...], to_row(gap) + to_row(own, seeds)], axis=1
        )
        line_ref[...] = jnp.broadcast_to(line[:, None, :], line_ref.shape)
    else:
        pack(wanted_ref, source, mass_slab(carry), message, message_hbm, send_sem)
        head_ref[...] = source[0]
        tail_ref[...] = source[blocks - 1]
    for c in range(parts):
        rank_store(c).wait()


def finish(last, vertices, devices, scalars, vectors, arrays, old=(), gaps=()):
    fetched = vectors[-1]
    banded, tiles, _ = arrays
    blocks, seeds, width = banded.shape
    shape = (seeds, blocks * width)
    operands = tuple(scalars) + tuple(vectors) + tuple(off_chip(x) for x in tuple(arrays) + tuple(old)) + tuple(gaps)
    if last:
        out_shape = (in_hbm(shape, F32), shaped((devices, 1, 256), F32))
        out_specs = (hbm(), vmem())
        scratch = [pltpu.SemaphoreType.DMA]
    else:
        edge = shaped((seeds, width), BF16)
        out_shape = (in_hbm(shape, F32), edge, edge, in_hbm(fetched.shape, BF16))
        out_specs = (hbm(), vmem(), vmem(), hbm())
        scratch = [
            VMEM((blocks, seeds, width), BF16),
            VMEM(fetched.shape, BF16),
            pltpu.SemaphoreType.DMA((4,)),
        ]
    return pl.pallas_call(
        functools.partial(finish_kernel, last, vertices),
        out_shape=out_shape,
        in_specs=[smem()] * len(scalars)
        + [vmem()] * len(vectors)
        + [hbm()] * (len(arrays) + len(old))
        + [vmem()] * len(gaps),
        out_specs=out_specs,
        scratch_shapes=scratch
        + [
            VMEM(tiles.shape, BF16),
            VMEM((blocks + 1, seeds, width), F32),
            VMEM((blocks, seeds, width), F32),
            VMEM(shape, F32),
            VMEM((2, width, width), BF16),
            pltpu.SemaphoreType.DMA((2,)),
            pltpu.SemaphoreType.DMA((tiles.shape[0] // UNROLL,)),
            pltpu.SemaphoreType.DMA,
            pltpu.SemaphoreType.DMA((8,)),
        ],
        compiler_params=PARAMS,
        name="finish",
    )(*operands)


def stats_kernel(seeds, vertices, group_ref, got_ref, change_ref, total_ref, own_ref):
    devices, _, lanes = got_ref.shape
    sums = [jnp.zeros((1, lanes), F32), jnp.zeros((1, lanes), F32)]
    for d in range(devices):
        sums[d % 2] = sums[d % 2] + got_ref[d]
    mine = jnp.where(group_ref[0] == 1, sums[1], sums[0])
    both = sums[0] + sums[1]
    for i in range(ITERS):
        at = slice(i * seeds, (i + 1) * seeds)
        change_ref[i : i + 1, :] = mine[:, at] / vertices
        total_ref[:, i : i + 1] = jnp.sum(both[:, at] / vertices, axis=1, keepdims=True) / (2 * seeds)
    own_ref[...] = mine[:, ITERS * seeds :]


def on_device(rank_in, band_tiles, off_tiles, tile_src, tile_row, tile_count, seed_ids, dangling):
    blocks, _, width, _ = band_tiles.shape
    seeds = rank_in.shape[0]
    peers = lax.axis_size("dom")
    devices = peers * lax.axis_size("seed")
    vertices = blocks * width * peers
    first = (lax.axis_index("dom") * (blocks * width)).astype(I32).reshape(1)
    group = lax.axis_index("seed").astype(I32).reshape(1)
    dangling = dangling.reshape(blocks, width)
    seeds_at = seed_ids.reshape(seeds, 1)

    request, slot, target = plan(tile_count, tile_src, tile_row, peers, blocks)
    wanted = lax.all_to_all(request, "dom", split_axis=0, concat_axis=0, tiled=True)
    source, slab, head, tail = prep(rank_in, dangling, blocks)
    message = pack_first(wanted, source, slab, peers)
    old, rank = None, rank_in
    gaps = []
    for iteration in range(ITERS):
        last = iteration + 1 == ITERS
        fetched = lax.all_to_all(message, "dom", split_axis=0, concat_axis=0, tiled=True)
        left = lax.ppermute(tail, "dom", [(i, i + 1) for i in range(peers - 1)])
        right = lax.ppermute(head, "dom", [(i + 1, i) for i in range(peers - 1)])
        gap_at = (iteration - 1) * seeds if iteration > 0 else None
        banded, *gap = band(gap_at, first, rank, old, band_tiles, dangling, seeds_at)
        gaps += gap
        scalars = (first, tile_count, slot, target, wanted)
        vectors = (seeds_at, dangling, left, right, fetched)
        arrays = (banded, off_tiles, band_tiles)
        if last:
            rank, line = finish(last, vertices, devices, scalars, vectors, arrays, (rank,), gaps)
        else:
            old = rank
            rank, head, tail, message = finish(last, vertices, devices, scalars, vectors, arrays)
    got = lax.all_to_all(line, ("dom", "seed"), split_axis=0, concat_axis=0, tiled=True)
    change, total, own = pl.pallas_call(
        functools.partial(stats_kernel, seeds, vertices),
        out_shape=(shaped((ITERS, seeds), F32), shaped((1, ITERS), F32), shaped((1, seeds), F32)),
        in_specs=[smem(), vmem()],
        out_specs=(vmem(),) * 3,
        compiler_params=SMALL,
        name="stats",
    )(group, got)
    return (rank, change, total.reshape(ITERS), own.reshape(seeds))


def solution(mesh):
    return jax.shard_map(
        on_device,
        mesh=mesh,
        in_specs=(
            P("seed", "dom"),
            P("dom", None, None, None),
            P("dom", None, None),
            P("dom", None),
            P("dom", None),
            P("dom"),
            P("seed"),
            P("dom"),
        ),
        out_specs=(P("seed", "dom"), P(None, "seed"), P(), P("seed")),
        check_vma=False,
    )
```

```python
import functools

import jax
import jax.numpy as jnp
from jax import lax
from jax.experimental import pallas as pl
from jax.experimental.pallas import tpu as pltpu
from jax.sharding import PartitionSpec as P

CAP = 2
ITERS = 3
DAMP = 0.85

BF16 = jnp.bfloat16
F32 = jnp.float32
I32 = jnp.int32
VMEM = pltpu.VMEM
NT = (((1,), (1,)), ((), ()))
SLAB = 8
PARAMS = pltpu.CompilerParams(vmem_limit_bytes=44 << 20)
MIDDLE = pltpu.CompilerParams(vmem_limit_bytes=34 << 20)
SMALL = pltpu.CompilerParams(vmem_limit_bytes=16 << 20)


def vmem():
    return pl.BlockSpec(memory_space=pltpu.VMEM)


def smem():
    return pl.BlockSpec(memory_space=pltpu.SMEM)


def hbm():
    return pl.BlockSpec(memory_space=pltpu.HBM)


def in_hbm(shape, dtype):
    return pltpu.HBM(shape, dtype)


def off_chip(x):
    return pltpu.with_memory_space_constraint(x, pltpu.HBM)


def shaped(shape, dtype):
    return jax.ShapeDtypeStruct(shape, dtype)


def dot_nt(x, w):
    return lax.dot_general(x, w, NT, preferred_element_type=F32)


def plan_kernel(peers, blocks, count_ref, src_ref, row_ref, request_ref, slot_ref, target_ref):
    slots = src_ref.shape[1]
    ids = src_ref[...]
    live = lax.broadcasted_iota(I32, (1, slots), 1) < count_ref[0]
    holder = ids // blocks
    inside = (ids - holder * blocks).astype(F32)
    peer = lax.broadcasted_iota(I32, (peers, slots), 0)
    held = jnp.broadcast_to(holder, (peers, slots)) == peer
    asked = jnp.logical_and(held, jnp.broadcast_to(live, (peers, slots)))
    block_of = jnp.broadcast_to(inside, (peers, slots))
    low = jnp.min(jnp.where(asked, block_of, float(blocks - 1)), axis=1, keepdims=True)
    high = jnp.max(jnp.where(asked, block_of, 0.0), axis=1, keepdims=True)
    lane = lax.broadcasted_iota(I32, request_ref.shape, 1)
    request_ref[...] = jnp.where(lane == 0, low, high).astype(I32)
    low_of = jnp.sum(jnp.where(held, low, 0.0), axis=0, keepdims=True)
    slot_ref[...] = holder * CAP + jnp.where(inside == low_of, 0, 1)
    target_ref[...] = jnp.where(live, row_ref[...], blocks)


def plan(tile_count, tile_src, tile_row, peers, blocks):
    slots = tile_src.shape[1]
    return pl.pallas_call(
        functools.partial(plan_kernel, peers, blocks),
        out_shape=(shaped((peers, 128), I32), shaped((1, slots), I32), shaped((1, slots), I32)),
        in_specs=[smem(), vmem(), vmem()],
        out_specs=(vmem(), vmem(), vmem()),
        name="plan",
    )(tile_count, tile_src, tile_row)


def eye(rows, start=0):
    lane = lax.broadcasted_iota(I32, (rows, 128), 1)
    return lax.broadcasted_iota(I32, (rows, 128), 0) + start == lane


def to_row(column, start=0):
    return jnp.sum(jnp.where(eye(column.shape[0], start), column, 0.0), axis=0, keepdims=True)


def to_column(row, seeds):
    return jnp.sum(jnp.where(eye(seeds), row, 0.0), axis=1, keepdims=True)


def mass_slab(mass):
    row = to_row(jnp.sum(mass, axis=1, keepdims=True))
    high = row.astype(BF16).astype(F32)
    rest = row - high
    middle = rest.astype(BF16).astype(F32)
    low = rest - middle
    at = lax.broadcasted_iota(I32, (SLAB, 128), 0)
    slab = jnp.where(at == 0, high, jnp.where(at == 1, middle, jnp.where(at == 2, low, 0.0)))
    return slab.astype(BF16)


def prep_kernel(rank_hbm, dangling_ref, source_ref, slab_ref, head_ref, tail_ref, rank, sem):
    blocks, seeds, width = source_ref.shape
    chunks = sem.shape[0]
    per = blocks // chunks

    def fetch(c):
        cols = pl.ds(c * per * width, per * width)
        return pltpu.make_async_copy(rank_hbm.at[:, cols], rank.at[:, cols], sem.at[c])

    for c in range(chunks):
        fetch(c).start()
    mass = jnp.zeros((seeds, width), F32)
    for c in range(chunks):
        fetch(c).wait()
        for b in range(c * per, (c + 1) * per):
            old = rank[:, b * width : (b + 1) * width]
            dead = jnp.broadcast_to(dangling_ref[b : b + 1, :], (seeds, width)) != 0
            kept = jnp.where(dead, 0.0, old)
            mass += old - kept
            source_ref[b] = kept.astype(BF16)
    slab_ref[...] = mass_slab(mass)
    head_ref[...] = source_ref[0]
    tail_ref[...] = source_ref[blocks - 1]


def prep(rank, dangling, blocks):
    seeds = rank.shape[0]
    width = rank.shape[1] // blocks
    edge = shaped((seeds, width), BF16)
    return pl.pallas_call(
        prep_kernel,
        out_shape=(shaped((blocks, seeds, width), BF16), shaped((SLAB, 128), BF16), edge, edge),
        in_specs=[hbm(), vmem()],
        out_specs=(vmem(),) * 4,
        scratch_shapes=[VMEM(rank.shape, F32), pltpu.SemaphoreType.DMA((8,))],
        compiler_params=SMALL,
        name="prep",
    )(off_chip(rank), dangling)


def pack(wanted, source, slab, message, out_hbm, sem):
    peers = message.shape[0]
    seeds = source.shape[1]
    parts = sem.shape[0]
    per = peers // parts

    def send(c):
        span = pl.ds(c * per, per)
        return pltpu.make_async_copy(message.at[span], out_hbm.at[span], sem.at[c])

    def one(p, carry):
        for k in range(CAP):
            message[p, k * seeds : (k + 1) * seeds, :] = source[wanted(p, k)]
        message[p, CAP * seeds :, :] = slab
        return carry

    for c in range(parts):
        lax.fori_loop(c * per, (c + 1) * per, one, 0, unroll=8)
        send(c).start()
    for c in range(parts):
        send(c).wait()


def pack_kernel(wanted_ref, source_ref, slab_ref, out_hbm, message, sem):
    pack(lambda p, k: wanted_ref[p, k], source_ref, slab_ref[...], message, out_hbm, sem)


def pack_first(wanted, source, slab, peers):
    _, seeds, width = source.shape
    shape = (peers, CAP * seeds + SLAB, width)
    return pl.pallas_call(
        pack_kernel,
        out_shape=in_hbm(shape, BF16),
        in_specs=[smem(), vmem(), vmem()],
        out_specs=hbm(),
        scratch_shapes=[VMEM(shape, BF16), pltpu.SemaphoreType.DMA((4,))],
        compiler_params=SMALL,
        name="pack",
    )(wanted, source, slab)


def from_seed(seed_ref, first_ref, width):
    seeds = seed_ref.shape[0]
    here = jnp.broadcast_to(seed_ref[...] - first_ref[0], (seeds, width))
    return here - lax.broadcasted_iota(I32, (seeds, width), 1)


def band_kernel(gap_at, first_ref, rank_hbm, *refs):
    refs = list(refs)
    old_hbm = None if gap_at is None else refs.pop(0)
    tiles_hbm, dangling_ref, seed_ref, out_hbm = refs[:4]
    refs = refs[4:]
    gap_ref = None if gap_at is None else refs.pop(0)
    rank, source, tiles, banded, sem, rank_sem, out_sem = refs[:7]
    blocks, seeds, width = banded.shape
    chunks = sem.shape[0]
    per = blocks // chunks

    def fetch(c):
        span = pl.ds(c * per, per)
        return pltpu.make_async_copy(tiles_hbm.at[span], tiles.at[span], sem.at[c])

    def flush(c):
        span = pl.ds(c * per, per)
        return pltpu.make_async_copy(banded.at[span], out_hbm.at[span], out_sem.at[c])

    def fetch_rank(c):
        cols = pl.ds(c * per * width, per * width)
        return pltpu.make_async_copy(rank_hbm.at[:, cols], rank.at[:, cols], rank_sem.at[c])

    def fetch_old(c):
        cols = pl.ds(c * per * width, per * width)
        return pltpu.make_async_copy(old_hbm.at[:, cols], refs[7].at[:, cols], refs[8].at[c])

    for c in range(chunks):
        fetch_rank(c).start()
        if gap_at is not None:
            fetch_old(c).start()
        fetch(c).start()

    gap = jnp.zeros((seeds, width), F32)

    def prepare(c, gap):
        fetch_rank(c).wait()
        if gap_at is not None:
            fetch_old(c).wait()
        for b in range(c * per, (c + 1) * per):
            cols = slice(b * width, (b + 1) * width)
            new = rank[:, cols]
            dead = jnp.broadcast_to(dangling_ref[b : b + 1, :], (seeds, width)) != 0
            source[b] = jnp.where(dead, 0.0, new).astype(BF16)
            if gap_at is not None:
                gap = gap + jnp.abs(new - refs[7][:, cols])
        return gap

    gap = prepare(0, gap)
    away = from_seed(seed_ref, first_ref, width)
    zero = jnp.zeros((seeds, width), BF16)
    for c in range(chunks):
        if c + 1 < chunks:
            gap = prepare(c + 1, gap)
        fetch(c).wait()
        for b in range(c * per, (c + 1) * per):
            before = source[b - 1] if b > 0 else zero
            after = source[b + 1] if b + 1 < blocks else zero
            x = jnp.concatenate([before, source[b], after], axis=1)
            w = jnp.concatenate([tiles[b, 0], tiles[b, 1], tiles[b, 2]], axis=1)
            banded[b] = DAMP * dot_nt(x, w) + jnp.where(away == b * width, 1.0 - DAMP, 0.0)
        flush(c).start()
    if gap_at is not None:
        gap_ref[...] = to_row(jnp.sum(gap, axis=1, keepdims=True), gap_at)
    for c in range(chunks):
        flush(c).wait()


def band(gap_at, first, rank, old, tiles, dangling, seeds_at):
    blocks, _, width, _ = tiles.shape
    seeds = rank.shape[0]
    shape = (blocks, seeds, width)
    ranks = [rank] if gap_at is None else [rank, old]
    out_shape = [in_hbm(shape, F32)]
    out_specs = [hbm()]
    extra = []
    if gap_at is not None:
        out_shape.append(shaped((1, 128), F32))
        out_specs.append(vmem())
        extra = [VMEM(rank.shape, F32), pltpu.SemaphoreType.DMA((8,))]
    return pl.pallas_call(
        functools.partial(band_kernel, gap_at),
        out_shape=tuple(out_shape),
        in_specs=[smem()] + [hbm()] * (len(ranks) + 1) + [vmem()] * 2,
        out_specs=tuple(out_specs),
        scratch_shapes=[
            VMEM(rank.shape, F32),
            VMEM(shape, BF16),
            VMEM(tiles.shape, BF16),
            VMEM(shape, F32),
            pltpu.SemaphoreType.DMA((8,)),
            pltpu.SemaphoreType.DMA((8,)),
            pltpu.SemaphoreType.DMA((8,)),
        ]
        + extra,
        compiler_params=MIDDLE,
        name="band",
    )(first, *(off_chip(x) for x in ranks), off_chip(tiles), dangling, seeds_at)


UNROLL = 64
DEPTH = 8


def finish_kernel(last, vertices, *refs):
    (first_ref, count_ref, slot_ref, target_ref, wanted_ref) = refs[:5]
    (seed_ref, dangling_ref, left_ref, right_ref, fetched) = refs[5:10]
    banded_hbm, tiles_hbm, band_hbm = refs[10:13]
    if last:
        rank_hbm, gap_one_ref, gap_two_ref, next_hbm, line_ref, rank_sem = refs[13:19]
        scratch = refs[19:]
    else:
        next_hbm, head_ref, tail_ref, message_hbm, source, message, send_sem = refs[13:20]
        scratch = refs[20:]
    tiles, acc, banded, rank, edges, edge_sem, tile_sem, base_sem, out_sem = scratch
    blocks, seeds, width = banded.shape
    parts = out_sem.shape[0]
    span = blocks // parts

    def edge_copy(k):
        at = band_hbm.at[0, 0] if k == 0 else band_hbm.at[blocks - 1, 2]
        return pltpu.make_async_copy(at, edges.at[k], edge_sem.at[k])

    def tile_copy(g):
        at = pl.ds(g * UNROLL, UNROLL)
        return pltpu.make_async_copy(tiles_hbm.at[at], tiles.at[at], tile_sem.at[g])

    def part_loads(c):
        at = pl.ds(c * span, span)
        loads = [pltpu.make_async_copy(banded_hbm.at[at], banded.at[at], base_sem.at[c])]
        if last:
            cols = pl.ds(c * span * width, span * width)
            loads.append(pltpu.make_async_copy(rank_hbm.at[:, cols], rank.at[:, cols], rank_sem.at[c]))
        return loads

    def rank_store(c):
        cols = pl.ds(c * span * width, span * width)
        return pltpu.make_async_copy(rank.at[:, cols], next_hbm.at[:, cols], out_sem.at[c])

    trips = (count_ref[0] + UNROLL - 1) // UNROLL
    for g in range(tile_sem.shape[0]):

        @pl.when(g < trips)
        def _():
            tile_copy(g).start()

    for k in range(2):
        edge_copy(k).start()
    for c in range(parts):
        for load in part_loads(c):
            load.start()
    mass_row = jnp.sum(jnp.sum(fetched[:, CAP * seeds :, :].astype(F32), axis=0), axis=0, keepdims=True)
    share = jnp.broadcast_to(DAMP * (to_column(mass_row, seeds) / vertices), (seeds, width))
    zero = jnp.zeros((seeds, width), BF16)
    acc[...] = jnp.zeros_like(acc)

    def operand(t):
        slot = slot_ref[0, t]
        at = pl.multiple_of((slot % CAP) * seeds, seeds)
        return fetched[slot // CAP, pl.ds(at, seeds), :]

    def group(g, carry):
        tile_copy(g).wait()
        first = g * UNROLL
        waiting = []

        def add(most):
            while len(waiting) > most:
                t, y = waiting.pop(0)
                for k in range(2):
                    row = target_ref[0, t + k]
                    acc[row] = acc[row] + y[k * seeds : (k + 1) * seeds]

        for u in range(0, UNROLL, 2):
            one, two = first + u, first + u + 1
            x = jnp.concatenate(
                [
                    jnp.concatenate([operand(one), zero], axis=1),
                    jnp.concatenate([zero, operand(two)], axis=1),
                ],
                axis=0,
            )
            waiting.append((one, dot_nt(x, jnp.concatenate([tiles[one], tiles[two]], axis=1))))
            add(DEPTH)
        add(0)
        return carry

    lax.fori_loop(0, trips, group, 0)
    for k in range(2):
        edge_copy(k).wait()
    acc[0] = acc[0] + dot_nt(left_ref[...], edges[0])
    acc[blocks - 1] = acc[blocks - 1] + dot_nt(right_ref[...], edges[1])
    if last:
        away = from_seed(seed_ref, first_ref, width)

    def update(b, carry):
        cols = pl.ds(pl.multiple_of(b * width, width), width)
        new = banded[b] + (DAMP * acc[b] + share)
        if last:
            gap, own = carry
            gap = gap + jnp.abs(new - rank[:, cols])
            rank[:, cols] = new
            return gap, own + jnp.where(away == b * width, new, 0.0)
        rank[:, cols] = new
        dead = jnp.broadcast_to(dangling_ref[pl.ds(b, 1), :], (seeds, width)) != 0
        kept = jnp.where(dead, 0.0, new)
        source[b] = kept.astype(BF16)
        return carry + (new - kept)

    nothing = jnp.zeros((seeds, width), F32)
    carry = (nothing, nothing) if last else nothing
    for c in range(parts):
        for load in part_loads(c):
            load.wait()
        carry = lax.fori_loop(c * span, (c + 1) * span, update, carry, unroll=8)
        rank_store(c).start()
    if last:
        gap, own = (jnp.sum(x, axis=1, keepdims=True) for x in carry)
        line = jnp.concatenate(
            [gap_one_ref[...] + gap_two_ref[...], to_row(gap) + to_row(own, seeds)], axis=1
        )
        line_ref[...] = jnp.broadcast_to(line[:, None, :], line_ref.shape)
    else:
        pack(lambda p, k: wanted_ref[k, p], source, mass_slab(carry), message, message_hbm, send_sem)
        head_ref[...] = source[0]
        tail_ref[...] = source[blocks - 1]
    for c in range(parts):
        rank_store(c).wait()


def finish(last, vertices, devices, scalars, vectors, arrays, old=(), gaps=()):
    fetched = vectors[-1]
    banded, tiles, _ = arrays
    blocks, seeds, width = banded.shape
    shape = (seeds, blocks * width)
    operands = tuple(scalars) + tuple(vectors) + tuple(off_chip(x) for x in tuple(arrays) + tuple(old)) + tuple(gaps)
    if last:
        out_shape = (in_hbm(shape, F32), shaped((devices, 1, 256), F32))
        out_specs = (hbm(), vmem())
        scratch = [pltpu.SemaphoreType.DMA((8,))]
    else:
        edge = shaped((seeds, width), BF16)
        out_shape = (in_hbm(shape, F32), edge, edge, in_hbm(fetched.shape, BF16))
        out_specs = (hbm(), vmem(), vmem(), hbm())
        scratch = [
            VMEM((blocks, seeds, width), BF16),
            VMEM(fetched.shape, BF16),
            pltpu.SemaphoreType.DMA((4,)),
        ]
    return pl.pallas_call(
        functools.partial(finish_kernel, last, vertices),
        out_shape=out_shape,
        in_specs=[smem()] * len(scalars)
        + [vmem()] * len(vectors)
        + [hbm()] * (len(arrays) + len(old))
        + [vmem()] * len(gaps),
        out_specs=out_specs,
        scratch_shapes=scratch
        + [
            VMEM(tiles.shape, BF16),
            VMEM((blocks + 1, seeds, width), F32),
            VMEM((blocks, seeds, width), F32),
            VMEM(shape, F32),
            VMEM((2, width, width), BF16),
            pltpu.SemaphoreType.DMA((2,)),
            pltpu.SemaphoreType.DMA((tiles.shape[0] // UNROLL,)),
            pltpu.SemaphoreType.DMA((8,)),
            pltpu.SemaphoreType.DMA((8,)),
        ],
        compiler_params=PARAMS,
        name="finish",
    )(*operands)


def stats_kernel(seeds, vertices, group_ref, got_ref, change_ref, total_ref, own_ref):
    devices, _, lanes = got_ref.shape
    sums = [jnp.zeros((1, lanes), F32), jnp.zeros((1, lanes), F32)]
    for d in range(devices):
        sums[d % 2] = sums[d % 2] + got_ref[d]
    mine = jnp.where(group_ref[0] == 1, sums[1], sums[0])
    both = sums[0] + sums[1]
    for i in range(ITERS):
        at = slice(i * seeds, (i + 1) * seeds)
        change_ref[i : i + 1, :] = mine[:, at] / vertices
        total_ref[:, i : i + 1] = jnp.sum(both[:, at] / vertices, axis=1, keepdims=True) / (2 * seeds)
    own_ref[...] = mine[:, ITERS * seeds :]


def on_device(rank_in, band_tiles, off_tiles, tile_src, tile_row, tile_count, seed_ids, dangling):
    blocks, _, width, _ = band_tiles.shape
    seeds = rank_in.shape[0]
    peers = lax.axis_size("dom")
    devices = peers * lax.axis_size("seed")
    vertices = blocks * width * peers
    first = (lax.axis_index("dom") * (blocks * width)).astype(I32).reshape(1)
    group = lax.axis_index("seed").astype(I32).reshape(1)
    dangling = dangling.reshape(blocks, width)
    seeds_at = seed_ids.reshape(seeds, 1)

    request, slot, target = plan(tile_count, tile_src, tile_row, peers, blocks)
    wanted = lax.all_to_all(request, "dom", split_axis=0, concat_axis=0, tiled=True)
    source, slab, head, tail = prep(rank_in, dangling, blocks)
    message = pack_first(wanted, source, slab, peers)
    asked = jnp.transpose(wanted[:, :CAP])
    old, rank = None, rank_in
    gaps = []
    for iteration in range(ITERS):
        last = iteration + 1 == ITERS
        fetched = lax.all_to_all(message, "dom", split_axis=0, concat_axis=0, tiled=True)
        left = lax.ppermute(tail, "dom", [(i, i + 1) for i in range(peers - 1)])
        right = lax.ppermute(head, "dom", [(i + 1, i) for i in range(peers - 1)])
        gap_at = (iteration - 1) * seeds if iteration > 0 else None
        banded, *gap = band(gap_at, first, rank, old, band_tiles, dangling, seeds_at)
        gaps += gap
        scalars = (first, tile_count, slot, target, asked)
        vectors = (seeds_at, dangling, left, right, fetched)
        arrays = (banded, off_tiles, band_tiles)
        if last:
            rank, line = finish(last, vertices, devices, scalars, vectors, arrays, (rank,), gaps)
        else:
            old = rank
            rank, head, tail, message = finish(last, vertices, devices, scalars, vectors, arrays)
    got = lax.all_to_all(line, ("dom", "seed"), split_axis=0, concat_axis=0, tiled=True)
    change, total, own = pl.pallas_call(
        functools.partial(stats_kernel, seeds, vertices),
        out_shape=(shaped((ITERS, seeds), F32), shaped((1, ITERS), F32), shaped((1, seeds), F32)),
        in_specs=[smem(), vmem()],
        out_specs=(vmem(),) * 3,
        compiler_params=SMALL,
        name="stats",
    )(group, got)
    return (rank, change, total.reshape(ITERS), own.reshape(seeds))


def solution(mesh):
    return jax.shard_map(
        on_device,
        mesh=mesh,
        in_specs=(
            P("seed", "dom"),
            P("dom", None, None, None),
            P("dom", None, None),
            P("dom", None),
            P("dom", None),
            P("dom"),
            P("seed"),
            P("dom"),
        ),
        out_specs=(P("seed", "dom"), P(None, "seed"), P(), P("seed")),
        check_vma=False,
    )
```

```python
import functools

import jax
import jax.numpy as jnp
from jax import lax
from jax.experimental import pallas as pl
from jax.experimental.pallas import tpu as pltpu
from jax.sharding import PartitionSpec as P

CAP = 2
ITERS = 3
DAMP = 0.85

BF16 = jnp.bfloat16
F32 = jnp.float32
I32 = jnp.int32
VMEM = pltpu.VMEM
NT = (((1,), (1,)), ((), ()))
SLAB = 8
PARAMS = pltpu.CompilerParams(vmem_limit_bytes=44 << 20)
MIDDLE = pltpu.CompilerParams(vmem_limit_bytes=34 << 20)
SMALL = pltpu.CompilerParams(vmem_limit_bytes=16 << 20)


def vmem():
    return pl.BlockSpec(memory_space=pltpu.VMEM)


def smem():
    return pl.BlockSpec(memory_space=pltpu.SMEM)


def hbm():
    return pl.BlockSpec(memory_space=pltpu.HBM)


def in_hbm(shape, dtype):
    return pltpu.HBM(shape, dtype)


def on_chip(shape, dtype):
    return pltpu.VMEM(shape, dtype)


def off_chip(x):
    return pltpu.with_memory_space_constraint(x, pltpu.HBM)


def shaped(shape, dtype):
    return jax.ShapeDtypeStruct(shape, dtype)


def dot_nt(x, w):
    return lax.dot_general(x, w, NT, preferred_element_type=F32)


def plan_kernel(peers, blocks, count_ref, src_ref, row_ref, request_ref, slot_ref, target_ref):
    slots = src_ref.shape[1]
    ids = src_ref[...]
    live = lax.broadcasted_iota(I32, (1, slots), 1) < count_ref[0]
    holder = ids // blocks
    inside = (ids - holder * blocks).astype(F32)
    peer = lax.broadcasted_iota(I32, (peers, slots), 0)
    held = jnp.broadcast_to(holder, (peers, slots)) == peer
    asked = jnp.logical_and(held, jnp.broadcast_to(live, (peers, slots)))
    block_of = jnp.broadcast_to(inside, (peers, slots))
    low = jnp.min(jnp.where(asked, block_of, float(blocks - 1)), axis=1, keepdims=True)
    high = jnp.max(jnp.where(asked, block_of, 0.0), axis=1, keepdims=True)
    lane = lax.broadcasted_iota(I32, request_ref.shape, 1)
    request_ref[...] = jnp.where(lane == 0, low, high).astype(I32)
    low_of = jnp.sum(jnp.where(held, low, 0.0), axis=0, keepdims=True)
    slot_ref[...] = holder * CAP + jnp.where(inside == low_of, 0, 1)
    target_ref[...] = jnp.where(live, row_ref[...], blocks)


def plan(tile_count, tile_src, tile_row, peers, blocks):
    slots = tile_src.shape[1]
    return pl.pallas_call(
        functools.partial(plan_kernel, peers, blocks),
        out_shape=(shaped((peers, 128), I32), shaped((1, slots), I32), shaped((1, slots), I32)),
        in_specs=[smem(), vmem(), vmem()],
        out_specs=(vmem(), vmem(), vmem()),
        name="plan",
    )(tile_count, tile_src, tile_row)


def eye(rows, start=0):
    lane = lax.broadcasted_iota(I32, (rows, 128), 1)
    return lax.broadcasted_iota(I32, (rows, 128), 0) + start == lane


def to_row(column, start=0):
    return jnp.sum(jnp.where(eye(column.shape[0], start), column, 0.0), axis=0, keepdims=True)


def to_column(row, seeds):
    return jnp.sum(jnp.where(eye(seeds), row, 0.0), axis=1, keepdims=True)


def mass_slab(mass):
    row = to_row(jnp.sum(mass, axis=1, keepdims=True))
    high = row.astype(BF16).astype(F32)
    rest = row - high
    middle = rest.astype(BF16).astype(F32)
    low = rest - middle
    at = lax.broadcasted_iota(I32, (SLAB, 128), 0)
    slab = jnp.where(at == 0, high, jnp.where(at == 1, middle, jnp.where(at == 2, low, 0.0)))
    return slab.astype(BF16)


def prep_kernel(rank_hbm, dangling_ref, source_ref, slab_ref, head_ref, tail_ref, rank, sem):
    blocks, seeds, width = source_ref.shape
    chunks = sem.shape[0]
    per = blocks // chunks

    def fetch(c):
        cols = pl.ds(c * per * width, per * width)
        return pltpu.make_async_copy(rank_hbm.at[:, cols], rank.at[:, cols], sem.at[c])

    for c in range(chunks):
        fetch(c).start()
    mass = jnp.zeros((seeds, width), F32)
    for c in range(chunks):
        fetch(c).wait()
        for b in range(c * per, (c + 1) * per):
            old = rank[:, b * width : (b + 1) * width]
            dead = jnp.broadcast_to(dangling_ref[b : b + 1, :], (seeds, width)) != 0
            kept = jnp.where(dead, 0.0, old)
            mass += old - kept
            source_ref[b] = kept.astype(BF16)
    slab_ref[...] = mass_slab(mass)
    head_ref[...] = source_ref[0]
    tail_ref[...] = source_ref[blocks - 1]


def prep(rank, dangling, blocks):
    seeds = rank.shape[0]
    width = rank.shape[1] // blocks
    edge = shaped((seeds, width), BF16)
    return pl.pallas_call(
        prep_kernel,
        out_shape=(shaped((blocks, seeds, width), BF16), shaped((SLAB, 128), BF16), edge, edge),
        in_specs=[hbm(), vmem()],
        out_specs=(vmem(),) * 4,
        scratch_shapes=[VMEM(rank.shape, F32), pltpu.SemaphoreType.DMA((8,))],
        compiler_params=SMALL,
        name="prep",
    )(off_chip(rank), dangling)


def pack(wanted, source, slab, message, out_hbm, sem):
    peers = message.shape[0]
    seeds = source.shape[1]
    parts = sem.shape[0]
    per = peers // parts

    def send(c):
        span = pl.ds(c * per, per)
        return pltpu.make_async_copy(message.at[span], out_hbm.at[span], sem.at[c])

    def one(p, carry):
        for k in range(CAP):
            message[p, k * seeds : (k + 1) * seeds, :] = source[wanted(p, k)]
        message[p, CAP * seeds :, :] = slab
        return carry

    for c in range(parts):
        lax.fori_loop(c * per, (c + 1) * per, one, 0, unroll=8)
        send(c).start()
    for c in range(parts):
        send(c).wait()


def pack_kernel(wanted_ref, source_ref, slab_ref, out_hbm, message, sem):
    pack(lambda p, k: wanted_ref[p, k], source_ref, slab_ref[...], message, out_hbm, sem)


def pack_first(wanted, source, slab, peers):
    _, seeds, width = source.shape
    shape = (peers, CAP * seeds + SLAB, width)
    return pl.pallas_call(
        pack_kernel,
        out_shape=in_hbm(shape, BF16),
        in_specs=[smem(), vmem(), vmem()],
        out_specs=hbm(),
        scratch_shapes=[VMEM(shape, BF16), pltpu.SemaphoreType.DMA((4,))],
        compiler_params=SMALL,
        name="pack",
    )(wanted, source, slab)


KEPT = 32


def from_seed(seed_ref, first_ref, width):
    seeds = seed_ref.shape[0]
    here = jnp.broadcast_to(seed_ref[...] - first_ref[0], (seeds, width))
    return here - lax.broadcasted_iota(I32, (seeds, width), 1)


def band_kernel(gap_at, first_ref, rank_hbm, *refs):
    refs = list(refs)
    old_hbm = None if gap_at is None else refs.pop(0)
    tiles_hbm, dangling_ref, seed_ref, out_hbm, kept_ref = refs[:5]
    refs = refs[5:]
    gap_ref = None if gap_at is None else refs.pop(0)
    rank, source, tiles, banded, sem, rank_sem, out_sem = refs[:7]
    blocks, seeds, width = banded.shape
    chunks = sem.shape[0]
    per = blocks // chunks

    def fetch(c):
        span = pl.ds(c * per, per)
        return pltpu.make_async_copy(tiles_hbm.at[span], tiles.at[span], sem.at[c])

    def flush(c):
        span = pl.ds(c * per, per)
        return pltpu.make_async_copy(banded.at[span], out_hbm.at[pl.ds(c * per - KEPT, per)], out_sem.at[c])

    def fetch_rank(c):
        cols = pl.ds(c * per * width, per * width)
        return pltpu.make_async_copy(rank_hbm.at[:, cols], rank.at[:, cols], rank_sem.at[c])

    def fetch_old(c):
        cols = pl.ds(c * per * width, per * width)
        return pltpu.make_async_copy(old_hbm.at[:, cols], refs[7].at[:, cols], refs[8].at[c])

    for c in range(chunks):
        fetch_rank(c).start()
        if gap_at is not None:
            fetch_old(c).start()
        fetch(c).start()

    gap = jnp.zeros((seeds, width), F32)

    def prepare(c, gap):
        fetch_rank(c).wait()
        if gap_at is not None:
            fetch_old(c).wait()
        for b in range(c * per, (c + 1) * per):
            cols = slice(b * width, (b + 1) * width)
            new = rank[:, cols]
            dead = jnp.broadcast_to(dangling_ref[b : b + 1, :], (seeds, width)) != 0
            source[b] = jnp.where(dead, 0.0, new).astype(BF16)
            if gap_at is not None:
                gap = gap + jnp.abs(new - refs[7][:, cols])
        return gap

    gap = prepare(0, gap)
    away = from_seed(seed_ref, first_ref, width)
    zero = jnp.zeros((seeds, width), BF16)
    for c in range(chunks):
        if c + 1 < chunks:
            gap = prepare(c + 1, gap)
        fetch(c).wait()
        for b in range(c * per, (c + 1) * per):
            before = source[b - 1] if b > 0 else zero
            after = source[b + 1] if b + 1 < blocks else zero
            x = jnp.concatenate([before, source[b], after], axis=1)
            w = jnp.concatenate([tiles[b, 0], tiles[b, 1], tiles[b, 2]], axis=1)
            into = kept_ref if b < KEPT else banded
            into[b] = DAMP * dot_nt(x, w) + jnp.where(away == b * width, 1.0 - DAMP, 0.0)
        if c * per >= KEPT:
            flush(c).start()
    if gap_at is not None:
        gap_ref[...] = to_row(jnp.sum(gap, axis=1, keepdims=True), gap_at)
    for c in range(KEPT // per, chunks):
        flush(c).wait()


def band(gap_at, first, rank, old, tiles, dangling, seeds_at):
    blocks, _, width, _ = tiles.shape
    seeds = rank.shape[0]
    shape = (blocks, seeds, width)
    ranks = [rank] if gap_at is None else [rank, old]
    out_shape = [in_hbm((blocks - KEPT, seeds, width), F32), on_chip((KEPT, seeds, width), F32)]
    out_specs = [hbm(), vmem()]
    extra = []
    if gap_at is not None:
        out_shape.append(shaped((1, 128), F32))
        out_specs.append(vmem())
        extra = [VMEM(rank.shape, F32), pltpu.SemaphoreType.DMA((8,))]
    return pl.pallas_call(
        functools.partial(band_kernel, gap_at),
        out_shape=tuple(out_shape),
        in_specs=[smem()] + [hbm()] * (len(ranks) + 1) + [vmem()] * 2,
        out_specs=tuple(out_specs),
        scratch_shapes=[
            VMEM(rank.shape, F32),
            VMEM(shape, BF16),
            VMEM(tiles.shape, BF16),
            VMEM(shape, F32),
            pltpu.SemaphoreType.DMA((8,)),
            pltpu.SemaphoreType.DMA((8,)),
            pltpu.SemaphoreType.DMA((8,)),
        ]
        + extra,
        compiler_params=MIDDLE,
        name="band",
    )(first, *(off_chip(x) for x in ranks), off_chip(tiles), dangling, seeds_at)


UNROLL = 64
DEPTH = 8


def finish_kernel(last, vertices, *refs):
    (first_ref, count_ref, slot_ref, target_ref, wanted_ref) = refs[:5]
    (seed_ref, dangling_ref, left_ref, right_ref, kept_ref, fetched) = refs[5:11]
    banded_hbm, tiles_hbm, band_hbm = refs[11:14]
    if last:
        rank_hbm, gap_one_ref, gap_two_ref, next_hbm, line_ref, rank_sem = refs[14:20]
        scratch = refs[20:]
    else:
        next_hbm, head_ref, tail_ref, message_hbm, source, message, send_sem = refs[14:21]
        scratch = refs[21:]
    tiles, acc, banded, rank, edges, edge_sem, tile_sem, base_sem, out_sem = scratch
    seeds, width = banded.shape[1:]
    blocks = banded.shape[0] + KEPT
    parts = out_sem.shape[0]
    span = blocks // parts

    def edge_copy(k):
        at = band_hbm.at[0, 0] if k == 0 else band_hbm.at[blocks - 1, 2]
        return pltpu.make_async_copy(at, edges.at[k], edge_sem.at[k])

    def tile_copy(g):
        at = pl.ds(g * UNROLL, UNROLL)
        return pltpu.make_async_copy(tiles_hbm.at[at], tiles.at[at], tile_sem.at[g])

    def part_loads(c):
        loads = []
        if c * span >= KEPT:
            at = pl.ds(c * span - KEPT, span)
            loads.append(pltpu.make_async_copy(banded_hbm.at[at], banded.at[at], base_sem.at[c]))
        if last:
            cols = pl.ds(c * span * width, span * width)
            loads.append(pltpu.make_async_copy(rank_hbm.at[:, cols], rank.at[:, cols], rank_sem.at[c]))
        return loads

    def rank_store(c):
        cols = pl.ds(c * span * width, span * width)
        return pltpu.make_async_copy(rank.at[:, cols], next_hbm.at[:, cols], out_sem.at[c])

    trips = (count_ref[0] + UNROLL - 1) // UNROLL
    for g in range(tile_sem.shape[0]):

        @pl.when(g < trips)
        def _():
            tile_copy(g).start()

    for k in range(2):
        edge_copy(k).start()
    for c in range(parts):
        for load in part_loads(c):
            load.start()
    mass_row = jnp.sum(jnp.sum(fetched[:, CAP * seeds :, :].astype(F32), axis=0), axis=0, keepdims=True)
    share = jnp.broadcast_to(DAMP * (to_column(mass_row, seeds) / vertices), (seeds, width))
    zero = jnp.zeros((seeds, width), BF16)
    acc[...] = jnp.zeros_like(acc)

    def operand(t):
        slot = slot_ref[0, t]
        at = pl.multiple_of((slot % CAP) * seeds, seeds)
        return fetched[slot // CAP, pl.ds(at, seeds), :]

    def group(g, carry):
        tile_copy(g).wait()
        first = g * UNROLL
        waiting = []

        def add(most):
            while len(waiting) > most:
                t, y = waiting.pop(0)
                for k in range(2):
                    row = target_ref[0, t + k]
                    acc[row] = acc[row] + y[k * seeds : (k + 1) * seeds]

        for u in range(0, UNROLL, 2):
            one, two = first + u, first + u + 1
            x = jnp.concatenate(
                [
                    jnp.concatenate([operand(one), zero], axis=1),
                    jnp.concatenate([zero, operand(two)], axis=1),
                ],
                axis=0,
            )
            waiting.append((one, dot_nt(x, jnp.concatenate([tiles[one], tiles[two]], axis=1))))
            add(DEPTH)
        add(0)
        return carry

    lax.fori_loop(0, trips, group, 0)
    for k in range(2):
        edge_copy(k).wait()
    acc[0] = acc[0] + dot_nt(left_ref[...], edges[0])
    acc[blocks - 1] = acc[blocks - 1] + dot_nt(right_ref[...], edges[1])
    if last:
        away = from_seed(seed_ref, first_ref, width)

    def update(kept_here, b, carry):
        cols = pl.ds(pl.multiple_of(b * width, width), width)
        base = kept_ref[b] if kept_here else banded[b - KEPT]
        new = base + (DAMP * acc[b] + share)
        if last:
            gap, own = carry
            gap = gap + jnp.abs(new - rank[:, cols])
            rank[:, cols] = new
            return gap, own + jnp.where(away == b * width, new, 0.0)
        rank[:, cols] = new
        dead = jnp.broadcast_to(dangling_ref[pl.ds(b, 1), :], (seeds, width)) != 0
        kept = jnp.where(dead, 0.0, new)
        source[b] = kept.astype(BF16)
        return carry + (new - kept)

    nothing = jnp.zeros((seeds, width), F32)
    carry = (nothing, nothing) if last else nothing
    for c in range(parts):
        for load in part_loads(c):
            load.wait()
        carry = lax.fori_loop(
            c * span, (c + 1) * span, functools.partial(update, c * span < KEPT), carry, unroll=8
        )
        rank_store(c).start()
    if last:
        gap, own = (jnp.sum(x, axis=1, keepdims=True) for x in carry)
        line = jnp.concatenate(
            [gap_one_ref[...] + gap_two_ref[...], to_row(gap) + to_row(own, seeds)], axis=1
        )
        line_ref[...] = jnp.broadcast_to(line[:, None, :], line_ref.shape)
    else:
        pack(lambda p, k: wanted_ref[k, p], source, mass_slab(carry), message, message_hbm, send_sem)
        head_ref[...] = source[0]
        tail_ref[...] = source[blocks - 1]
    for c in range(parts):
        rank_store(c).wait()


def finish(last, vertices, devices, scalars, vectors, arrays, old=(), gaps=()):
    fetched = vectors[-1]
    banded, tiles, _ = arrays
    seeds, width = banded.shape[1:]
    blocks = banded.shape[0] + KEPT
    shape = (seeds, blocks * width)
    operands = tuple(scalars) + tuple(vectors) + tuple(off_chip(x) for x in tuple(arrays) + tuple(old)) + tuple(gaps)
    if last:
        out_shape = (in_hbm(shape, F32), shaped((devices, 1, 256), F32))
        out_specs = (hbm(), vmem())
        scratch = [pltpu.SemaphoreType.DMA((8,))]
    else:
        edge = shaped((seeds, width), BF16)
        out_shape = (in_hbm(shape, F32), edge, edge, in_hbm(fetched.shape, BF16))
        out_specs = (hbm(), vmem(), vmem(), hbm())
        scratch = [
            VMEM((blocks, seeds, width), BF16),
            VMEM(fetched.shape, BF16),
            pltpu.SemaphoreType.DMA((4,)),
        ]
    return pl.pallas_call(
        functools.partial(finish_kernel, last, vertices),
        out_shape=out_shape,
        in_specs=[smem()] * len(scalars)
        + [vmem()] * len(vectors)
        + [hbm()] * (len(arrays) + len(old))
        + [vmem()] * len(gaps),
        out_specs=out_specs,
        scratch_shapes=scratch
        + [
            VMEM(tiles.shape, BF16),
            VMEM((blocks + 1, seeds, width), F32),
            VMEM(banded.shape, F32),
            VMEM(shape, F32),
            VMEM((2, width, width), BF16),
            pltpu.SemaphoreType.DMA((2,)),
            pltpu.SemaphoreType.DMA((tiles.shape[0] // UNROLL,)),
            pltpu.SemaphoreType.DMA((8,)),
            pltpu.SemaphoreType.DMA((8,)),
        ],
        compiler_params=PARAMS,
        name="finish",
    )(*operands)


def stats_kernel(seeds, vertices, group_ref, got_ref, change_ref, total_ref, own_ref):
    devices, _, lanes = got_ref.shape
    sums = [jnp.zeros((1, lanes), F32), jnp.zeros((1, lanes), F32)]
    for d in range(devices):
        sums[d % 2] = sums[d % 2] + got_ref[d]
    mine = jnp.where(group_ref[0] == 1, sums[1], sums[0])
    both = sums[0] + sums[1]
    for i in range(ITERS):
        at = slice(i * seeds, (i + 1) * seeds)
        change_ref[i : i + 1, :] = mine[:, at] / vertices
        total_ref[:, i : i + 1] = jnp.sum(both[:, at] / vertices, axis=1, keepdims=True) / (2 * seeds)
    own_ref[...] = mine[:, ITERS * seeds :]


def on_device(rank_in, band_tiles, off_tiles, tile_src, tile_row, tile_count, seed_ids, dangling):
    blocks, _, width, _ = band_tiles.shape
    seeds = rank_in.shape[0]
    peers = lax.axis_size("dom")
    devices = peers * lax.axis_size("seed")
    vertices = blocks * width * peers
    first = (lax.axis_index("dom") * (blocks * width)).astype(I32).reshape(1)
    group = lax.axis_index("seed").astype(I32).reshape(1)
    dangling = dangling.reshape(blocks, width)
    seeds_at = seed_ids.reshape(seeds, 1)

    request, slot, target = plan(tile_count, tile_src, tile_row, peers, blocks)
    wanted = lax.all_to_all(request, "dom", split_axis=0, concat_axis=0, tiled=True)
    source, slab, head, tail = prep(rank_in, dangling, blocks)
    message = pack_first(wanted, source, slab, peers)
    asked = jnp.transpose(wanted[:, :CAP])
    old, rank = None, rank_in
    gaps = []
    for iteration in range(ITERS):
        last = iteration + 1 == ITERS
        fetched = lax.all_to_all(message, "dom", split_axis=0, concat_axis=0, tiled=True)
        left = lax.ppermute(tail, "dom", [(i, i + 1) for i in range(peers - 1)])
        right = lax.ppermute(head, "dom", [(i + 1, i) for i in range(peers - 1)])
        gap_at = (iteration - 1) * seeds if iteration > 0 else None
        banded, kept, *gap = band(gap_at, first, rank, old, band_tiles, dangling, seeds_at)
        gaps += gap
        scalars = (first, tile_count, slot, target, asked)
        vectors = (seeds_at, dangling, left, right, kept, fetched)
        arrays = (banded, off_tiles, band_tiles)
        if last:
            rank, line = finish(last, vertices, devices, scalars, vectors, arrays, (rank,), gaps)
        else:
            old = rank
            rank, head, tail, message = finish(last, vertices, devices, scalars, vectors, arrays)
    got = lax.all_to_all(line, ("dom", "seed"), split_axis=0, concat_axis=0, tiled=True)
    change, total, own = pl.pallas_call(
        functools.partial(stats_kernel, seeds, vertices),
        out_shape=(shaped((ITERS, seeds), F32), shaped((1, ITERS), F32), shaped((1, seeds), F32)),
        in_specs=[smem(), vmem()],
        out_specs=(vmem(),) * 3,
        compiler_params=SMALL,
        name="stats",
    )(group, got)
    return (rank, change, total.reshape(ITERS), own.reshape(seeds))


def solution(mesh):
    return jax.shard_map(
        on_device,
        mesh=mesh,
        in_specs=(
            P("seed", "dom"),
            P("dom", None, None, None),
            P("dom", None, None),
            P("dom", None),
            P("dom", None),
            P("dom"),
            P("seed"),
            P("dom"),
        ),
        out_specs=(P("seed", "dom"), P(None, "seed"), P(), P("seed")),
        check_vma=False,
    )
```
